128 devices in a mesh: req: 32 (over z, x, core), tp: 4 (over y).
Axes of the slice: x: 4, y: 4, z: 4, core: 2. Of those that a mesh axis runs over, the one named last changes fastest.
Arguments:
- tokens: bfloat16 [16384, 2048], P('req', 'tp'), may hold values from -6 to 6
- first_gain: float32 [2048], replicated, may hold values from 0.5 to 1.5
- first_shift: float32 [2048], replicated, may hold values from -2.5 to 2.5
- project_weight: bfloat16 [2048, 3, 2048], P(None, None, 'tp'), may hold values from -0.125 to 0.125
- project_bias: float32 [3, 2048], P(None, 'tp'), may hold values from -3 to 3
- output_weight: bfloat16 [2048, 2048], P('tp'), may hold values from -0.125 to 0.125
- second_gain: float32 [2048], replicated, may hold values from 0.5 to 1.5
- second_shift: float32 [2048], replicated, may hold values from -2.5 to 2.5
- expand_weight: bfloat16 [2048, 2, 3072], P(None, None, 'tp'), may hold values from -0.125 to 0.125
- contract_weight: bfloat16 [3072, 2048], P('tp'), may hold values from -0.109375 to 0.109375
- prior_cache: bfloat16 [32, 1024, 2, 2048], P('req', None, None, 'tp'), may hold values from -21 to 21
- prior_len: int32 [32], replicated, may hold values from 16 to 1024, as said below
- slot_map: int32 [32], replicated, may hold values from 0 to 31, each once
- block_table: int32 [32, 6], replicated, may hold values from 0 to 11, as said below
Outputs:
- mixed_out: bfloat16 [16384, 2048], P('req', 'tp')
- page_pool: bfloat16 [32, 12, 256, 2, 1024], P('req', None, None, None, 'tp')
The draws below stay inside these ranges and needn't reach their ends.
Inputs may be any that keep to these rules, and one draw needn't show every extreme that they name: `prior_len`: every request has at least 16 cached positions; some request has exactly 1024. `block_table`: rows 2g and 2g+1 together name each of the 12 pages exactly once.
All inputs are finite; a program needn't handle non-finite values.
Results may differ from the reference program's by a relative error of at most 0.018.
Values may be sent and summed in bfloat16 or wider, within the bound.
No kernel may reach another device: no remote copies, remote signals or barrier semaphores. Data moves between devices by JAX's collectives and lax.ppermute only.
A program may use at most 128 MiB of HBM per device.

```python
import jax
import jax.numpy as jnp
from jax import lax

D = 2048
HEADS = 32
HEAD_DIM = 64
ROTARY = 16
FF = 3072
STRETCH = 512
BLOCK = 256
MAX_PRIOR = 1024
REQUESTS = 32
TOKENS = 16384
BLOCKS = 6
PAGES = 12
N_TP = 4


def draw_project_bias(key, part):
    base_draw = jnp.clip(0.5 * jax.random.normal(jax.random.fold_in(key, 11), (3, HEADS, HEAD_DIM), jnp.float32), -2.5, 2.5)
    return base_draw.reshape(3, HEADS * HEAD_DIM)


def draw_prior_cache(key, part):
    normal_draw = jnp.clip(jax.random.normal(jax.random.fold_in(key, 12), (REQUESTS, MAX_PRIOR, 2, HEADS, HEAD_DIM), jnp.float32), -6.0, 6.0)
    return normal_draw.reshape(REQUESTS, MAX_PRIOR, 2, HEADS * HEAD_DIM).astype(jnp.bfloat16)


def draw_prior_len(key, part):
    lengths = jax.random.randint(jax.random.fold_in(key, 14), (REQUESTS,), 16, MAX_PRIOR + 1, jnp.int32)
    longest = jax.random.randint(jax.random.fold_in(key, 15), (), 0, REQUESTS, jnp.int32)
    return lengths.at[longest].set(MAX_PRIOR)


def draw_block_table(key, part):
    group_keys = jax.random.split(jax.random.fold_in(key, 16), REQUESTS // 2)
    page_perms = jax.vmap(lambda group_key: jax.random.permutation(group_key, PAGES))(group_keys)
    return page_perms.reshape(REQUESTS, BLOCKS).astype(jnp.int32)


def levels(key, shape, shards, low, top_value):
    factor_of, own = 1.0, jax.random.fold_in(key, 6)
    for axis_at, shards_of in shards:
        heights = jnp.exp(jax.random.uniform(jax.random.fold_in(own, axis_at), (shards_of,), jnp.float32, low / len(shards), top_value / len(shards)))
        factor_of = factor_of * jnp.repeat(heights, shape[axis_at] // shards_of).reshape([-1 if axis == axis_at else 1 for axis in range(len(shape))])
    return factor_of


def bell_draw(own_key, shape, deviation, limit, pieces=(), kind=jnp.bfloat16):
    drawn = deviation * jax.random.normal(own_key, shape, jnp.float32)
    if pieces:
        drawn = drawn * levels(own_key, shape, pieces, -0.22, 0.18)
    return jnp.clip(drawn, -limit, limit).astype(kind)


def setup_inputs(seed: int = 0) -> dict:
    arg_keys = jax.random.split(jax.random.key(seed), 15)
    tokens = bell_draw(arg_keys[0], (TOKENS, D), 1.0, 6.0, ((0, 32), (1, 4)))
    first_gain = jnp.clip(1.0 + 0.1 * jax.random.normal(arg_keys[1], (D,), jnp.float32), 0.5, 1.5)
    first_shift = bell_draw(arg_keys[2], (D,), 0.3, 2.5, (), jnp.float32)
    project_weight = bell_draw(arg_keys[3], (D, 3, HEADS * HEAD_DIM), D ** -0.5, 0.125, ((2, 4),))
    project_bias = draw_project_bias(jax.random.fold_in(arg_keys[14], 71), 0)
    output_weight = bell_draw(arg_keys[5], (HEADS * HEAD_DIM, D), (HEADS * HEAD_DIM) ** -0.5, 0.125, ((0, 4),))
    second_gain = jnp.clip(1.0 + 0.1 * jax.random.normal(arg_keys[6], (D,), jnp.float32), 0.5, 1.5)
    second_shift = bell_draw(arg_keys[7], (D,), 0.3, 2.5, (), jnp.float32)
    expand_weight = bell_draw(arg_keys[8], (D, 2, FF), D ** -0.5, 0.125, ((2, 4),))
    contract_weight = bell_draw(arg_keys[9], (FF, D), FF ** -0.5, 0.109375, ((0, 4),))
    prior_cache = draw_prior_cache(jax.random.fold_in(arg_keys[14], 71), 0)
    prior_len = draw_prior_len(jax.random.fold_in(arg_keys[14], 71), 0)
    slot_map = jax.random.permutation(arg_keys[12], REQUESTS).astype(jnp.int32)
    block_table = draw_block_table(jax.random.fold_in(arg_keys[14], 71), 0)
    return {"tokens": tokens, "first_gain": first_gain, "first_shift": first_shift, "project_weight": project_weight, "project_bias": project_bias, "output_weight": output_weight, "second_gain": second_gain, "second_shift": second_shift, "expand_weight": expand_weight, "contract_weight": contract_weight, "prior_cache": prior_cache, "prior_len": prior_len, "slot_map": slot_map, "block_table": block_table}


EPSILON = 1e-05
ROPE_BASE = 10000.0
MASK_FILL = -1e+30

def layer_norm(inputs, gain_row, shift_row):
    center = inputs - lax.optimization_barrier(jnp.mean(inputs, axis=-1, keepdims=True))
    spread = lax.optimization_barrier(jnp.mean(center * center, axis=-1, keepdims=True))
    return (center * lax.rsqrt(spread + EPSILON) * gain_row + shift_row).astype(jnp.bfloat16)

def rotate(values, positions):
    half_rot = ROTARY // 2
    frequency = ROPE_BASE ** (-2.0 * jnp.arange(half_rot, dtype=jnp.float32) / ROTARY)
    angles = positions.astype(jnp.float32)[:, None] * frequency[None, :]
    cosine = jnp.cos(angles)[:, None, :]
    sine_part = jnp.sin(angles)[:, None, :]
    first_half = values[..., :half_rot]
    second_half = values[..., half_rot:ROTARY]
    return jnp.concatenate([first_half * cosine - second_half * sine_part, second_half * cosine + first_half * sine_part, values[..., ROTARY:]], axis=-1)

def attend(queries, key_rows, value_rows, prior_count):
    query_count = queries.shape[0]
    cache_rows = key_rows.shape[0] - query_count
    scores = jnp.einsum('qhd,khd->hqk', queries.astype(jnp.float32), key_rows.astype(jnp.float32)) * HEAD_DIM ** (-0.5)
    key_index = jnp.arange(key_rows.shape[0], dtype=jnp.int32)[None, :]
    query_index = jnp.arange(query_count, dtype=jnp.int32)[:, None]
    allowed = jnp.where(key_index < cache_rows, key_index < prior_count, key_index - cache_rows <= query_index)
    scores = jnp.where(allowed[None], scores, MASK_FILL)
    highest = lax.optimization_barrier(jnp.max(scores, axis=-1, keepdims=True))
    weights = jnp.exp(scores - highest)
    normalized = (weights / lax.optimization_barrier(jnp.sum(weights, axis=-1, keepdims=True))).astype(jnp.bfloat16)
    mixture = jnp.einsum('hqk,khd->qhd', normalized.astype(jnp.float32), value_rows.astype(jnp.float32))
    return mixture.astype(jnp.bfloat16)

def summed_parts(left_rows, right_rows):
    block_width = left_rows.shape[1] // N_TP
    summed = jnp.zeros((left_rows.shape[0], right_rows.shape[1]), jnp.float32)
    for part_index in range(N_TP):
        partial_term = jnp.dot(left_rows[:, part_index * block_width:(part_index + 1) * block_width], right_rows[part_index * block_width:(part_index + 1) * block_width], preferred_element_type=jnp.float32)
        partial_term = lax.optimization_barrier(partial_term.astype(jnp.bfloat16))
        summed = summed + partial_term.astype(jnp.float32)
    return summed

def assemble(prior_part, new_part, prior_count):
    padded = jnp.concatenate([prior_part, jnp.zeros(new_part.shape, prior_part.dtype)], axis=0)
    return lax.dynamic_update_slice(padded, new_part, (prior_count, jnp.int32(0), jnp.int32(0)))

def reference(tokens, first_gain, first_shift, project_weight, project_bias, output_weight, second_gain, second_shift, expand_weight, contract_weight, prior_cache, prior_len, slot_map, block_table):
    full_width = HEADS * HEAD_DIM
    project_flat = project_weight.reshape(D, 3 * full_width)
    expand_flat = expand_weight.reshape(D, 2 * FF)

    def one_request(operands):
        token_rows, cached, prior_count = operands
        stretch_len = token_rows.shape[0]
        inputs = token_rows.astype(jnp.float32)
        normed = layer_norm(inputs, first_gain, first_shift)
        projected = jnp.dot(normed, project_flat, preferred_element_type=jnp.float32).reshape(stretch_len, 3, full_width) + project_bias
        positions = prior_count + jnp.arange(stretch_len, dtype=jnp.int32)
        queries = rotate(projected[:, 0].reshape(stretch_len, HEADS, HEAD_DIM), positions).astype(jnp.bfloat16)
        new_keys = rotate(projected[:, 1].reshape(stretch_len, HEADS, HEAD_DIM), positions).astype(jnp.bfloat16)
        new_values = projected[:, 2].reshape(stretch_len, HEADS, HEAD_DIM).astype(jnp.bfloat16)
        key_rows = jnp.concatenate([cached[:, 0].reshape(MAX_PRIOR, HEADS, HEAD_DIM), new_keys], axis=0)
        value_rows = jnp.concatenate([cached[:, 1].reshape(MAX_PRIOR, HEADS, HEAD_DIM), new_values], axis=0)
        mixture = attend(queries, key_rows, value_rows, prior_count).reshape(stretch_len, full_width)
        residual = (inputs + summed_parts(mixture, output_weight)).astype(jnp.bfloat16)
        second_normed = layer_norm(residual.astype(jnp.float32), second_gain, second_shift)
        gate_up = jnp.dot(second_normed, expand_flat, preferred_element_type=jnp.float32).reshape(stretch_len, 2, FF)
        hidden = (jax.nn.silu(gate_up[:, 0]) * gate_up[:, 1]).astype(jnp.bfloat16)
        result = (residual.astype(jnp.float32) + summed_parts(hidden, contract_weight)).astype(jnp.bfloat16)
        kept_rows = jnp.arange(MAX_PRIOR, dtype=jnp.int32)[:, None, None] < prior_count
        masked = jnp.where(kept_rows, cached, jnp.zeros((), jnp.bfloat16))
        fresh_cache = jnp.stack([new_keys.reshape(stretch_len, full_width), new_values.reshape(stretch_len, full_width)], axis=1)
        return (result, assemble(masked, fresh_cache, prior_count))
    outputs, caches = lax.map(one_request, (tokens.reshape(REQUESTS, STRETCH, D), prior_cache, prior_len))
    half_width = full_width // 2
    local_half = half_width // N_TP
    groups = REQUESTS // 2
    inverse = jnp.zeros((REQUESTS,), jnp.int32).at[slot_map].set(jnp.arange(REQUESTS, dtype=jnp.int32))
    by_slot = caches[inverse].reshape(REQUESTS, BLOCKS, BLOCK, 2, N_TP, 2, local_half)
    by_slot = by_slot.transpose(0, 5, 1, 2, 3, 4, 6).reshape(groups, 2, 2, BLOCKS, BLOCK, 2, half_width)
    page_items = by_slot.transpose(0, 2, 1, 3, 4, 5, 6).reshape(REQUESTS, 2 * BLOCKS, BLOCK, 2, half_width)
    page_ids = jnp.broadcast_to(block_table.reshape(groups, 1, 2 * BLOCKS), (groups, 2, 2 * BLOCKS)).reshape(REQUESTS, 2 * BLOCKS)
    owners = jnp.broadcast_to(jnp.arange(REQUESTS, dtype=jnp.int32)[:, None], page_ids.shape)
    page_pool = jnp.zeros((REQUESTS, PAGES, BLOCK, 2, half_width), jnp.bfloat16).at[owners, page_ids].set(page_items)
    return (outputs.reshape(TOKENS, D), page_pool)
```

```python
import functools

import jax
import jax.numpy as jnp
from jax import lax
from jax.experimental import pallas as pl
from jax.experimental.pallas import tpu as pltpu
from jax.sharding import PartitionSpec as P

HEAD_DIM = 64
ROTARY = 16
BLOCK = 256
EPSILON = 1e-05
ROPE_BASE = 10000.0
MASK_FILL = -1e30
BF = jnp.bfloat16
F32 = jnp.float32


OFFSETS = (0, 3, 1, 2)


def shift_by(value, step):
    return lax.ppermute(value, "tp", [(i, (i + step) % 4) for i in range(4)])


def ring_gather(share):
    half = share.shape[0] // 2
    top, bottom = share[:half], share[half:]
    left_top = shift_by(top, 1)
    right_bottom = shift_by(bottom, -1)
    left_bottom = shift_by(bottom, 1)
    right_top = shift_by(top, -1)
    far_top = shift_by(left_top, 1)
    far_bottom = shift_by(right_bottom, -1)
    return (share[:half], share[half:], left_top, left_bottom, right_top, right_bottom, far_top, far_bottom)


def ring_scatter(parts):
    half = parts.shape[1] // 2
    add = lambda a, b: (a.astype(F32) + b.astype(F32))
    far_top = shift_by(parts[3, :half], 1)
    far_bottom = shift_by(parts[3, half:], -1)
    from_left_bottom = shift_by(parts[2, half:], 1)
    from_right_top = shift_by(parts[1, :half], -1)
    from_left_top = shift_by(add(parts[2, :half], far_top).astype(BF), 1)
    from_right_bottom = shift_by(add(parts[1, half:], far_bottom).astype(BF), -1)
    top = add(parts[0, :half], from_right_top) + from_left_top.astype(F32)
    bottom = add(parts[0, half:], from_left_bottom) + from_right_bottom.astype(F32)
    return jnp.concatenate([top, bottom], axis=0)


def norm_into(normed, pieces, gain, shift, blocks, half):
    width = pieces[0].shape[1]
    total = 4 * width
    step = 64
    for part in range(2):
        refs = pieces[part::2]

        def body(index, carry, refs=refs, part=part):
            at = pl.multiple_of(index * step, step)
            rows = [ref[pl.ds(at, step), :].astype(F32) for ref in refs]
            mean = sum(jnp.sum(row, axis=1, keepdims=True) for row in rows) / total
            rows = [row - mean for row in rows]
            spread = sum(jnp.sum(row * row, axis=1, keepdims=True) for row in rows) / total
            scale = lax.rsqrt(spread + EPSILON)
            for slot, row in enumerate(rows):
                line = blocks[slot]
                value = row * scale * gain[pl.ds(line, 1), :] + shift[pl.ds(line, 1), :]
                normed[pl.ds(part * half + at, step), slot * width : (slot + 1) * width] = value.astype(BF)
            return carry

        lax.fori_loop(0, half // step, body, 0)


def project_kernel(
    place, o0, o1, l0, l1, r0, r1, f0, f1, gain, shift, weight, bias, cosine, sine_a, sine_b, queries, keys, values, buffer, normed, sems
):
    device = place[0]
    width = o0.shape[1]
    half = o0.shape[0]
    blocks = [lax.rem(device + offset, 4) for offset in OFFSETS]
    copies = []
    for slot in range(4):
        copies.append(
            pltpu.make_async_copy(
                weight.at[:, pl.ds(blocks[slot] * width, width), :],
                buffer.at[:, pl.ds(slot * width, width), :],
                sems.at[slot],
            )
        )
        copies[-1].start()
    norm_into(normed, (o0, o1, l0, l1, r0, r1, f0, f1), gain, shift, blocks, half)
    for copy in copies:
        copy.wait()
    outs = (queries, keys, values)
    for part in range(2):
        rows = slice(part * half, (part + 1) * half)
        for which in range(3):
            product = jnp.dot(normed[rows, :], buffer[which], preferred_element_type=F32)
            product = product + bias[which : which + 1, :]
            if which == 2:
                outs[which][rows, :] = product.astype(BF)
                continue
            for tile in range(width // 128):
                lanes = slice(tile * 128, (tile + 1) * 128)
                value = product[:, lanes]
                up = pltpu.roll(value, 128 - ROTARY // 2, 1)
                down = pltpu.roll(value, ROTARY // 2, 1)
                turned = value * cosine[rows, :] + up * sine_a[rows, :] + down * sine_b[rows, :]
                if which == 0:
                    turned = turned * HEAD_DIM ** (-0.5)
                outs[which][rows, lanes] = turned.astype(BF)


VMEM = pltpu.MemorySpace.VMEM
SMEM = pltpu.MemorySpace.SMEM


def specs(*kinds):
    table = {"v": pl.BlockSpec(memory_space=VMEM), "s": pl.BlockSpec(memory_space=SMEM), "a": pl.BlockSpec(memory_space=pl.ANY)}
    return [table[kind] for kind in kinds]


PARAMS = pltpu.CompilerParams(vmem_limit_bytes=56 * 1024 * 1024)


def project(device, pieces, gain, shift, weight, bias, tables):
    half, width = pieces[0].shape
    out = jax.ShapeDtypeStruct((2 * half, width), BF)
    return pl.pallas_call(
        project_kernel,
        out_shape=(out, out, out),
        in_specs=specs("s", *"v" * 8, "v", "v", "a", "v", "v", "v", "v"),
        out_specs=tuple(specs("v", "v", "v")),
        scratch_shapes=[
            pltpu.VMEM((3, 4 * width, width), BF),
            pltpu.VMEM((2 * half, 4 * width), BF),
            pltpu.SemaphoreType.DMA((4,)),
        ],
        compiler_params=PARAMS,
        name="project",
    )(device, *pieces, gain, shift, weight, bias, *tables)


def attend_kernel(place, queries, new_keys, new_values, old_keys, old_values, weight, out, buffer, mixed, sems):
    device = place[0]
    prior = place[1]
    rows_all, width = queries.shape
    cached = old_keys.shape[0]
    blocks = [lax.rem(device + offset, 4) for offset in OFFSETS]
    copies = []
    for slot in range(4):
        copies.append(
            pltpu.make_async_copy(
                weight.at[:, pl.ds(blocks[slot] * width, width)], buffer.at[:, slot * width : (slot + 1) * width], sems.at[slot]
            )
        )
        copies[-1].start()
    step = 256
    contract = (((1,), (1,)), ((), ()))
    for part in range(rows_all // step):
        rows = slice(part * step, (part + 1) * step)
        seen = (part + 1) * step

        def body(pair, carry, rows=rows, seen=seen, part=part):
            lanes = pl.ds(pl.multiple_of(pair * 128, 128), 128)
            query = queries[rows, lanes]
            old_key, new_key = old_keys[:, lanes], new_keys[:seen, lanes]
            old_value, new_value = old_values[:, lanes], new_values[:seen, lanes]
            lane = lax.broadcasted_iota(jnp.int32, (step, 128), 1)
            old_allowed = lax.broadcasted_iota(jnp.int32, (1, cached), 1) < prior
            new_allowed = lax.broadcasted_iota(jnp.int32, (step, seen), 1) <= lax.broadcasted_iota(
                jnp.int32, (step, seen), 0
            ) + part * step
            results = []
            for head in range(2):
                own = (lane < HEAD_DIM) if head == 0 else (lane >= HEAD_DIM)
                masked = jnp.where(own, query, jnp.zeros((), BF))
                old_score = lax.dot_general(masked, old_key, contract, preferred_element_type=F32)
                old_score = jnp.where(old_allowed, old_score, MASK_FILL)
                new_score = lax.dot_general(masked, new_key, contract, preferred_element_type=F32)
                new_score = jnp.where(new_allowed, new_score, MASK_FILL)
                highest = jnp.maximum(
                    jnp.max(old_score, axis=1, keepdims=True), jnp.max(new_score, axis=1, keepdims=True)
                )
                old_weight = jnp.exp(old_score - highest)
                new_weight = jnp.exp(new_score - highest)
                total = jnp.sum(old_weight, axis=1, keepdims=True) + jnp.sum(new_weight, axis=1, keepdims=True)
                value = jnp.dot(old_weight.astype(BF), old_value, preferred_element_type=F32) + jnp.dot(
                    new_weight.astype(BF), new_value, preferred_element_type=F32
                )
                results.append(value / total)
            mixed[rows, lanes] = jnp.where(lane < HEAD_DIM, results[0], results[1]).astype(BF)
            return carry

        lax.fori_loop(0, width // 128, body, 0)
    for copy in copies:
        copy.wait()
    for part in range(rows_all // step):
        rows = slice(part * step, (part + 1) * step)
        for slot in range(4):
            product = jnp.dot(mixed[rows, :], buffer[:, slot * width : (slot + 1) * width], preferred_element_type=F32)
            out[slot, rows, :] = product.astype(BF)


def attend(place, queries, new_keys, new_values, old_keys, old_values, weight):
    rows, width = queries.shape
    return pl.pallas_call(
        attend_kernel,
        out_shape=jax.ShapeDtypeStruct((4, rows, width), BF),
        in_specs=specs("s", "v", "v", "v", "v", "v", "a"),
        out_specs=specs("v")[0],
        scratch_shapes=[pltpu.VMEM((width, 4 * width), BF), pltpu.VMEM((rows, width), BF), pltpu.SemaphoreType.DMA((4,))],
        compiler_params=PARAMS,
        name="attend",
    )(place, queries, new_keys, new_values, old_keys, old_values, weight)


def forward_kernel(
    place, o0, o1, l0, l1, r0, r1, f0, f1, gain, shift, expand, contract, out, expand_buffer, contract_buffer, normed, sems
):
    device = place[0]
    half, width = o0.shape
    blocks = [lax.rem(device + offset, 4) for offset in OFFSETS]
    copies = []
    for slot in range(4):
        copies.append(
            pltpu.make_async_copy(
                expand.at[:, pl.ds(blocks[slot] * width, width), :],
                expand_buffer.at[:, slot * width : (slot + 1) * width, :],
                sems.at[0, slot],
            )
        )
    for slot in range(4):
        copies.append(
            pltpu.make_async_copy(
                contract.at[:, pl.ds(blocks[slot] * width, width)],
                contract_buffer.at[:, slot * width : (slot + 1) * width],
                sems.at[1, slot],
            )
        )
    for copy in copies:
        copy.start()
    norm_into(normed, (o0, o1, l0, l1, r0, r1, f0, f1), gain, shift, blocks, half)
    for copy in copies:
        copy.wait()
    for part in range(2):
        rows = slice(part * half, (part + 1) * half)
        gate = jnp.dot(normed[rows, :], expand_buffer[0], preferred_element_type=F32)
        up = jnp.dot(normed[rows, :], expand_buffer[1], preferred_element_type=F32)
        hidden = (gate / (1.0 + jnp.exp(-gate)) * up).astype(BF)
        for slot in range(4):
            product = jnp.dot(hidden, contract_buffer[:, slot * width : (slot + 1) * width], preferred_element_type=F32)
            out[slot, rows, :] = product.astype(BF)


def feed_forward(device, pieces, gain, shift, expand, contract):
    half, width = pieces[0].shape
    hidden = expand.shape[2]
    return pl.pallas_call(
        forward_kernel,
        out_shape=jax.ShapeDtypeStruct((4, 2 * half, width), BF),
        in_specs=specs("s", *"v" * 8, "v", "v", "a", "a"),
        out_specs=specs("v")[0],
        scratch_shapes=[
            pltpu.VMEM((2, 4 * width, hidden), BF),
            pltpu.VMEM((hidden, 4 * width), BF),
            pltpu.VMEM((2 * half, 4 * width), BF),
            pltpu.SemaphoreType.DMA((2, 4)),
        ],
        compiler_params=PARAMS,
        name="feed_forward",
    )(device, *pieces, gain, shift, expand, contract)


def reorder_kernel(owners, pieces, out, sem):
    count, rows, _, width = pieces.shape
    half = width // 2

    def body(slot, carry):
        group = slot // 2
        for side in range(2):
            pltpu.make_async_copy(
                pieces.at[owners[slot], :, :, side * half : (side + 1) * half],
                out.at[2 * group + side, slot - 2 * group],
                sem,
            ).start()
        return carry

    lax.fori_loop(0, count, body, 0)
    pltpu.make_async_copy(out, out, sem).wait()


def reorder(owners, pieces):
    count, rows, _, width = pieces.shape
    return pl.pallas_call(
        reorder_kernel,
        out_shape=jax.ShapeDtypeStruct((count, 2, rows, 2, width // 2), BF),
        in_specs=specs("s", "a"),
        out_specs=specs("a")[0],
        scratch_shapes=[pltpu.SemaphoreType.DMA],
        compiler_params=PARAMS,
        name="reorder",
    )(owners, pieces)


def pages_kernel(lengths, table, old, new, out, full, blank, sems):
    count, _, old_rows, _, width = old.shape
    new_rows = new.shape[2]
    cached, fresh = count * old_rows, count * new_rows
    blank[...] = jnp.zeros(blank.shape, BF)
    for slot in range(2):

        def load(index, carry, slot=slot):
            pltpu.make_async_copy(
                old.at[index, slot], full.at[slot, pl.ds(index * old_rows, old_rows)], sems.at[0, slot]
            ).start()
            return carry

        lax.fori_loop(0, count, load, 0)
    for slot in range(2):
        whole = full.at[slot, pl.ds(0, cached)]
        pltpu.make_async_copy(whole, whole, sems.at[0, slot]).wait()
        length = lengths[slot]

        def fill(index, carry, slot=slot, length=length):
            pltpu.make_async_copy(
                blank, full.at[slot, pl.ds(length + fresh + index * BLOCK, BLOCK)], sems.at[1, slot]
            ).start()
            return carry

        lax.fori_loop(0, cached // BLOCK, fill, 0)

        def store(index, carry, slot=slot, length=length):
            pltpu.make_async_copy(
                new.at[index, slot], full.at[slot, pl.ds(length + index * new_rows, new_rows)], sems.at[1, slot]
            ).start()
            return carry

        lax.fori_loop(0, count, store, 0)
    for slot in range(2):
        whole = full.at[slot, pl.ds(0, cached + fresh)]
        pltpu.make_async_copy(whole, whole, sems.at[1, slot]).wait()
        for block in range((cached + fresh) // BLOCK):
            pltpu.make_async_copy(
                full.at[slot, pl.ds(block * BLOCK, BLOCK)],
                out.at[0, table[slot * ((cached + fresh) // BLOCK) + block]],
                sems.at[2, 0],
            ).start()
    pltpu.make_async_copy(out, out, sems.at[2, 0]).wait()


def pages(lengths, table, old, new):
    count, _, old_rows, _, width = old.shape
    cached, fresh = count * old_rows, count * new.shape[2]
    return pl.pallas_call(
        pages_kernel,
        out_shape=jax.ShapeDtypeStruct((1, 2 * (cached + fresh) // BLOCK, BLOCK, 2, width), BF),
        in_specs=specs("s", "s", "a", "a"),
        out_specs=specs("a")[0],
        scratch_shapes=[
            pltpu.VMEM((2, 2 * cached + fresh, 2, width), BF),
            pltpu.VMEM((BLOCK, 2, width), BF),
            pltpu.SemaphoreType.DMA((3, 2)),
        ],
        compiler_params=PARAMS,
        name="pages",
    )(lengths, table, old, new)


def rotary_tables(prior_count, rows):
    lane = jnp.arange(128, dtype=jnp.int32) % HEAD_DIM
    half_rot = ROTARY // 2
    frequency = ROPE_BASE ** (-2.0 * (lane % half_rot).astype(F32) / ROTARY)
    frequency = jnp.where(lane < ROTARY, frequency, 0.0)
    positions = (prior_count + jnp.arange(rows, dtype=jnp.int32)).astype(F32)
    angles = positions[:, None] * frequency[None, :]
    sine = jnp.sin(angles)
    return (
        jnp.cos(angles),
        jnp.where(lane < half_rot, -sine, 0.0),
        jnp.where((lane >= half_rot) & (lane < ROTARY), sine, 0.0),
    )


def exchange(pieces):
    return lax.all_to_all(pieces, "req", split_axis=0, concat_axis=0, tiled=True)


def local(
    tokens,
    first_gain,
    first_shift,
    project_weight,
    project_bias,
    output_weight,
    second_gain,
    second_shift,
    expand_weight,
    contract_weight,
    prior_cache,
    prior_len,
    slot_map,
    block_table,
):
    request = lax.axis_index("req")
    device = lax.axis_index("tp").astype(jnp.int32)
    count = slot_map.shape[0]
    prior_count = prior_len[request]
    rows, width = tokens.shape
    cached = prior_cache.shape[1]
    owners = jnp.sum(
        jnp.where(
            slot_map[None, :] == jnp.arange(count, dtype=jnp.int32)[:, None], jnp.arange(count, dtype=jnp.int32)[None, :], 0
        ),
        axis=1,
        dtype=jnp.int32,
    )
    group = request // 2
    own_slots = lax.dynamic_slice_in_dim(owners, 2 * group, 2, 0)
    lengths = jnp.sum(
        jnp.where(own_slots[:, None] == jnp.arange(count, dtype=jnp.int32)[None, :], prior_len[None, :], 0), axis=1, dtype=jnp.int32
    )
    table = lax.dynamic_slice_in_dim(block_table, 2 * group, 2, 0).reshape(-1)
    place = jnp.stack([device, prior_count]).astype(jnp.int32)

    old = exchange(prior_cache.reshape(count, cached // count, 2, width))
    old = exchange(reorder(owners, old))

    pieces = ring_gather(tokens)
    tables = rotary_tables(prior_count, rows)
    weight = jnp.transpose(project_weight, (1, 0, 2))
    queries, new_keys, new_values = project(
        place, pieces, first_gain.reshape(4, width), first_shift.reshape(4, width), weight, project_bias, tables
    )
    fresh = jnp.stack([new_keys, new_values], axis=1)
    new = exchange(fresh.reshape(count, rows // count, 2, width))
    new = exchange(reorder(owners, new))

    old_keys, old_values = prior_cache[0, :, 0], prior_cache[0, :, 1]
    parts = attend(place, queries, new_keys, new_values, old_keys, old_values, output_weight)
    residual = (tokens.astype(F32) + ring_scatter(parts)).astype(BF)
    pieces = ring_gather(residual)
    parts = feed_forward(
        place,
        pieces,
        second_gain.reshape(4, width),
        second_shift.reshape(4, width),
        jnp.transpose(expand_weight, (1, 0, 2)),
        contract_weight,
    )
    result = (residual.astype(F32) + ring_scatter(parts)).astype(BF)
    page_pool = pages(lengths, table, old, new)
    return (result, page_pool)


def solution(mesh):
    return jax.shard_map(
        local,
        mesh=mesh,
        in_specs=(
            P("req", "tp"),
            P(),
            P(),
            P(None, None, "tp"),
            P(None, "tp"),
            P("tp", None),
            P(),
            P(),
            P(None, None, "tp"),
            P("tp", None),
            P("req", None, None, "tp"),
            P(),
            P(),
            P(),
        ),
        out_specs=(P("req", "tp"), P("req", None, None, None, "tp")),
        check_vma=False,
    )
```

```python
import jax
import jax.numpy as jnp
from jax import lax
from jax.experimental import pallas as pl
from jax.experimental.pallas import tpu as pltpu
from jax.sharding import PartitionSpec as P


HEAD_DIM = 64
ROTARY = 16
BLOCK = 256
EPSILON = 1e-05
ROPE_BASE = 10000.0
MASK_FILL = -1e30
BF = jnp.bfloat16
F32 = jnp.float32


OFFSETS = (0, 3, 1, 2)


def shift_by(value, step):
    return lax.ppermute(value, "tp", [(i, (i + step) % 4) for i in range(4)])


def ring_gather(top, bottom):
    left_top = shift_by(top, 1)
    right_bottom = shift_by(bottom, -1)
    left_bottom = shift_by(bottom, 1)
    right_top = shift_by(top, -1)
    far_top = shift_by(left_top, 1)
    far_bottom = shift_by(right_bottom, -1)
    return (top, bottom, left_top, left_bottom, right_top, right_bottom, far_top, far_bottom)


def ring_scatter(parts):
    own_top, own_bottom, left_top, left_bottom, right_top, right_bottom, far_top, far_bottom = parts
    add = lambda a, b: (a.astype(F32) + b.astype(F32))
    far_top = shift_by(far_top, 1)
    far_bottom = shift_by(far_bottom, -1)
    from_left_bottom = shift_by(right_bottom, 1)
    from_right_top = shift_by(left_top, -1)
    from_left_top = shift_by(add(right_top, far_top).astype(BF), 1)
    from_right_bottom = shift_by(add(left_bottom, far_bottom).astype(BF), -1)
    top = add(own_top, from_right_top) + from_left_top.astype(F32)
    bottom = add(own_bottom, from_left_bottom) + from_right_bottom.astype(F32)
    return top, bottom


def norm_into(normed, pieces, gain, shift, blocks, half):
    width = pieces[0].shape[1]
    total = 4 * width
    step = 64
    for part in range(2):
        refs = pieces[part::2]

        def body(index, carry, refs=refs, part=part):
            at = pl.multiple_of(index * step, step)
            rows = [ref[pl.ds(at, step), :].astype(F32) for ref in refs]
            mean = sum(jnp.sum(row, axis=1, keepdims=True) for row in rows) / total
            rows = [row - mean for row in rows]
            spread = sum(jnp.sum(row * row, axis=1, keepdims=True) for row in rows) / total
            scale = lax.rsqrt(spread + EPSILON)
            for slot, row in enumerate(rows):
                line = blocks[slot]
                value = row * scale * gain[pl.ds(line, 1), :] + shift[pl.ds(line, 1), :]
                normed[pl.ds(part * half + at, step), slot * width : (slot + 1) * width] = value.astype(BF)
            return carry

        lax.fori_loop(0, half // step, body, 0)


def project_kernel(
    o0, o1, l0, l1, r0, r1, f0, f1, gain, shift, weight, bias, cosine, sine_a, sine_b, queries, keys, values, buffer, normed, sems
):
    device = lax.axis_index("tp")
    width = o0.shape[1]
    half = o0.shape[0]
    blocks = [lax.rem(device + offset, 4) for offset in OFFSETS]
    copies = []
    for slot in range(4):
        copies.append(
            pltpu.make_async_copy(
                weight.at[:, pl.ds(blocks[slot] * width, width), :],
                buffer.at[:, pl.ds(slot * width, width), :],
                sems.at[slot],
            )
        )
        copies[-1].start()
    norm_into(normed, (o0, o1, l0, l1, r0, r1, f0, f1), gain, shift, blocks, half)
    for copy in copies:
        copy.wait()
    outs = (queries, keys, values)
    for part in range(2):
        rows = slice(part * half, (part + 1) * half)
        for which in range(3):
            product = jnp.dot(normed[rows, :], buffer[which], preferred_element_type=F32)
            product = product + bias[which : which + 1, :]
            if which == 2:
                outs[which][rows, :] = product.astype(BF)
                continue
            for tile in range(width // 128):
                lanes = slice(tile * 128, (tile + 1) * 128)
                value = product[:, lanes]
                up = pltpu.roll(value, 128 - ROTARY // 2, 1)
                down = pltpu.roll(value, ROTARY // 2, 1)
                turned = value * cosine[rows, :] + up * sine_a[rows, :] + down * sine_b[rows, :]
                if which == 0:
                    turned = turned * HEAD_DIM ** (-0.5)
                outs[which][rows, lanes] = turned.astype(BF)


VMEM = pltpu.MemorySpace.VMEM
SMEM = pltpu.MemorySpace.SMEM


def specs(*kinds):
    table = {"v": pl.BlockSpec(memory_space=VMEM), "s": pl.BlockSpec(memory_space=SMEM), "a": pl.BlockSpec(memory_space=pl.ANY)}
    return [table[kind] for kind in kinds]


PARAMS = pltpu.CompilerParams(vmem_limit_bytes=56 * 1024 * 1024)


def project(pieces, gain, shift, weight, bias, tables):
    half, width = pieces[0].shape
    out = jax.ShapeDtypeStruct((2 * half, width), BF)
    return pl.pallas_call(
        project_kernel,
        out_shape=(out, out, out),
        in_specs=specs(*"v" * 8, "v", "v", "a", "v", "v", "v", "v"),
        out_specs=tuple(specs("v", "v", "v")),
        scratch_shapes=[
            pltpu.VMEM((3, 4 * width, width), BF),
            pltpu.VMEM((2 * half, 4 * width), BF),
            pltpu.SemaphoreType.DMA((4,)),
        ],
        compiler_params=PARAMS,
        name="project",
    )(*pieces, gain, shift, weight, bias, *tables)


def attend_kernel(lengths, queries, new_keys, new_values, old_keys, old_values, weight, *refs):
    outs, (buffer, mixed, sems) = refs[:8], refs[8:]
    device = lax.axis_index("tp")
    prior = lengths[lax.axis_index("req")]
    rows_all, width = queries.shape
    cached = old_keys.shape[0]
    blocks = [lax.rem(device + offset, 4) for offset in OFFSETS]
    copies = []
    for slot in range(4):
        copies.append(
            pltpu.make_async_copy(
                weight.at[:, pl.ds(blocks[slot] * width, width)], buffer.at[:, slot * width : (slot + 1) * width], sems.at[slot]
            )
        )
        copies[-1].start()
    step = 256
    contract = (((1,), (1,)), ((), ()))
    for part in range(rows_all // step):
        rows = slice(part * step, (part + 1) * step)
        seen = (part + 1) * step

        def body(pair, carry, rows=rows, seen=seen, part=part):
            lanes = pl.ds(pl.multiple_of(pair * 128, 128), 128)
            query = queries[rows, lanes]
            old_key, new_key = old_keys[:, lanes], new_keys[:seen, lanes]
            old_value, new_value = old_values[:, lanes], new_values[:seen, lanes]
            lane = lax.broadcasted_iota(jnp.int32, (step, 128), 1)
            old_allowed = lax.broadcasted_iota(jnp.int32, (1, cached), 1) < prior
            new_allowed = lax.broadcasted_iota(jnp.int32, (step, seen), 1) <= lax.broadcasted_iota(
                jnp.int32, (step, seen), 0
            ) + part * step
            results = []
            for head in range(2):
                own = (lane < HEAD_DIM) if head == 0 else (lane >= HEAD_DIM)
                masked = jnp.where(own, query, jnp.zeros((), BF))
                old_score = lax.dot_general(masked, old_key, contract, preferred_element_type=F32)
                old_score = jnp.where(old_allowed, old_score, MASK_FILL)
                new_score = lax.dot_general(masked, new_key, contract, preferred_element_type=F32)
                new_score = jnp.where(new_allowed, new_score, MASK_FILL)
                highest = jnp.maximum(
                    jnp.max(old_score, axis=1, keepdims=True), jnp.max(new_score, axis=1, keepdims=True)
                )
                old_weight = jnp.exp(old_score - highest)
                new_weight = jnp.exp(new_score - highest)
                total = jnp.sum(old_weight, axis=1, keepdims=True) + jnp.sum(new_weight, axis=1, keepdims=True)
                value = jnp.dot(old_weight.astype(BF), old_value, preferred_element_type=F32) + jnp.dot(
                    new_weight.astype(BF), new_value, preferred_element_type=F32
                )
                results.append(value / total)
            mixed[rows, lanes] = jnp.where(lane < HEAD_DIM, results[0], results[1]).astype(BF)
            return carry

        lax.fori_loop(0, width // 128, body, 0)
    for copy in copies:
        copy.wait()
    for part in range(rows_all // step):
        rows = slice(part * step, (part + 1) * step)
        for slot in range(4):
            product = jnp.dot(mixed[rows, :], buffer[:, slot * width : (slot + 1) * width], preferred_element_type=F32)
            outs[2 * slot + part][...] = product.astype(BF)


def attend(lengths, queries, new_keys, new_values, old_keys, old_values, weight):
    rows, width = queries.shape
    return pl.pallas_call(
        attend_kernel,
        out_shape=(jax.ShapeDtypeStruct((rows // 2, width), BF),) * 8,
        in_specs=specs("s", "v", "v", "v", "v", "v", "a"),
        out_specs=tuple(specs(*"v" * 8)),
        scratch_shapes=[pltpu.VMEM((width, 4 * width), BF), pltpu.VMEM((rows, width), BF), pltpu.SemaphoreType.DMA((4,))],
        compiler_params=PARAMS,
        name="attend",
    )(lengths, queries, new_keys, new_values, old_keys, old_values, weight)


def forward_kernel(o0, o1, l0, l1, r0, r1, f0, f1, gain, shift, expand, contract, *refs):
    outs, (expand_buffer, contract_buffer, normed, sems) = refs[:8], refs[8:]
    device = lax.axis_index("tp")
    half, width = o0.shape
    blocks = [lax.rem(device + offset, 4) for offset in OFFSETS]
    copies = []
    for slot in range(4):
        copies.append(
            pltpu.make_async_copy(
                expand.at[:, pl.ds(blocks[slot] * width, width), :],
                expand_buffer.at[:, slot * width : (slot + 1) * width, :],
                sems.at[0, slot],
            )
        )
    for slot in range(4):
        copies.append(
            pltpu.make_async_copy(
                contract.at[:, pl.ds(blocks[slot] * width, width)],
                contract_buffer.at[:, slot * width : (slot + 1) * width],
                sems.at[1, slot],
            )
        )
    for copy in copies:
        copy.start()
    norm_into(normed, (o0, o1, l0, l1, r0, r1, f0, f1), gain, shift, blocks, half)
    for copy in copies:
        copy.wait()
    for part in range(2):
        rows = slice(part * half, (part + 1) * half)
        gate = jnp.dot(normed[rows, :], expand_buffer[0], preferred_element_type=F32)
        up = jnp.dot(normed[rows, :], expand_buffer[1], preferred_element_type=F32)
        hidden = (gate / (1.0 + jnp.exp(-gate)) * up).astype(BF)
        for slot in range(4):
            product = jnp.dot(hidden, contract_buffer[:, slot * width : (slot + 1) * width], preferred_element_type=F32)
            outs[2 * slot + part][...] = product.astype(BF)


def feed_forward(pieces, gain, shift, expand, contract):
    half, width = pieces[0].shape
    hidden = expand.shape[2]
    return pl.pallas_call(
        forward_kernel,
        out_shape=(jax.ShapeDtypeStruct((half, width), BF),) * 8,
        in_specs=specs(*"v" * 8, "v", "v", "a", "a"),
        out_specs=tuple(specs(*"v" * 8)),
        scratch_shapes=[
            pltpu.VMEM((2, 4 * width, hidden), BF),
            pltpu.VMEM((hidden, 4 * width), BF),
            pltpu.VMEM((2 * half, 4 * width), BF),
            pltpu.SemaphoreType.DMA((2, 4)),
        ],
        compiler_params=PARAMS,
        name="feed_forward",
    )(*pieces, gain, shift, expand, contract)


def split_kernel(cache, keys, values):
    _, _, width = cache.shape
    step = 128
    row = lax.broadcasted_iota(jnp.int32, (2 * step, 2 * step), 0)
    column = lax.broadcasted_iota(jnp.int32, (2 * step, 2 * step), 1)
    source = jnp.where(row < step, 2 * row, 2 * (row - step) + 1)
    chosen = jnp.where(column == source, 1.0, 0.0).astype(BF)

    def body(index, carry):
        at = pl.multiple_of(index * step, step)
        pair = cache[pl.ds(at, step)].reshape(2 * step, width)
        parted = jnp.dot(chosen, pair, preferred_element_type=F32).astype(BF)
        keys[pl.ds(at, step), :] = parted[:step]
        values[pl.ds(at, step), :] = parted[step:]
        return carry

    lax.fori_loop(0, cache.shape[0] // step, body, 0)


def split(cache):
    rows, _, width = cache.shape
    out = jax.ShapeDtypeStruct((rows, width), BF)
    return pl.pallas_call(
        split_kernel,
        out_shape=(out, out),
        in_specs=specs("v"),
        out_specs=tuple(specs("v", "v")),
        compiler_params=PARAMS,
        name="split",
    )(cache)


def find_owners(slot_map, owners):
    def body(index, carry):
        owners[slot_map[index]] = index
        return carry

    lax.fori_loop(0, slot_map.shape[0], body, 0)


def mix_kernel(slot_map, pieces, keys, values, out, owners, stage, sems):
    count, rows, _, width = pieces.shape
    half = width // 2
    fresh = keys.shape[0] // count
    find_owners(slot_map, owners)

    def send(slot, carry):
        group = slot // 2
        for side in range(2):
            pltpu.make_async_copy(
                pieces.at[owners[slot], :, :, side * half : (side + 1) * half],
                out.at[2 * group + side, pl.ds((slot - 2 * group) * rows, rows)],
                sems.at[0],
            ).start()
        return carry

    lax.fori_loop(0, count, send, 0)

    def weave(slot, carry):
        at = pl.multiple_of(slot * fresh, fresh)
        for side in range(2):
            lanes = slice(side * half, (side + 1) * half)
            stage[slot, side * fresh : (side + 1) * fresh, 0, :] = keys[pl.ds(at, fresh), lanes]
            stage[slot, side * fresh : (side + 1) * fresh, 1, :] = values[pl.ds(at, fresh), lanes]
        return carry

    lax.fori_loop(0, count, weave, 0)
    last = pltpu.make_async_copy(stage, out.at[:, 2 * rows :], sems.at[1])
    last.start()
    first = out.at[:, : 2 * rows]
    pltpu.make_async_copy(first, first, sems.at[0]).wait()
    last.wait()


def mix(slot_map, pieces, keys, values):
    count, rows, _, width = pieces.shape
    fresh = keys.shape[0] // count
    return pl.pallas_call(
        mix_kernel,
        out_shape=jax.ShapeDtypeStruct((count, 2 * rows + 2 * fresh, 2, width // 2), BF),
        in_specs=specs("s", "v", "v", "v"),
        out_specs=specs("a")[0],
        scratch_shapes=[
            pltpu.SMEM((count,), jnp.int32),
            pltpu.VMEM((count, 2 * fresh, 2, width // 2), BF),
            pltpu.SemaphoreType.DMA((2,)),
        ],
        compiler_params=PARAMS,
        name="mix",
    )(slot_map, pieces, keys, values)


def reorder_kernel(slot_map, mixed, out, owners, sem):
    count, rows, _, _ = mixed.shape
    fresh = out.shape[2]
    find_owners(slot_map, owners)

    def send(slot, carry):
        group = slot // 2
        for side in range(2):
            pltpu.make_async_copy(
                mixed.at[owners[slot], pl.ds(rows - (2 - side) * fresh, fresh)],
                out.at[2 * group + side, slot - 2 * group],
                sem,
            ).start()
        return carry

    lax.fori_loop(0, count, send, 0)
    pltpu.make_async_copy(out, out, sem).wait()


def reorder(slot_map, mixed, fresh):
    count, _, _, width = mixed.shape
    return pl.pallas_call(
        reorder_kernel,
        out_shape=jax.ShapeDtypeStruct((count, 2, fresh, 2, width), BF),
        in_specs=specs("s", "a"),
        out_specs=specs("v")[0],
        scratch_shapes=[pltpu.SMEM((count,), jnp.int32), pltpu.SemaphoreType.DMA],
        compiler_params=PARAMS,
        name="reorder",
    )(slot_map, mixed)


def pages_kernel(slot_map, prior_len, table, mixed, new, out, owners, full, blank, sems):
    count, _, new_rows, _, _ = new.shape
    old_rows = (mixed.shape[1] - 2 * new_rows) // 2
    cached, fresh = count * old_rows, count * new_rows
    blocks = (cached + fresh) // BLOCK
    group = lax.axis_index("req") // 2
    find_owners(slot_map, owners)
    for slot in range(2):

        def load(index, carry, slot=slot):
            pltpu.make_async_copy(
                mixed.at[index, pl.ds(slot * old_rows, old_rows)], full.at[slot, pl.ds(index * old_rows, old_rows)], sems.at[0, slot]
            ).start()
            return carry

        lax.fori_loop(0, count, load, 0)
    blank[...] = jnp.zeros(blank.shape, BF)
    for slot in range(2):
        whole = full.at[slot, pl.ds(0, cached)]
        pltpu.make_async_copy(whole, whole, sems.at[0, slot]).wait()
        length = prior_len[owners[2 * group + slot]]

        def fill(index, carry, slot=slot, length=length):
            pltpu.make_async_copy(
                blank, full.at[slot, pl.ds(length + fresh + index * BLOCK, BLOCK)], sems.at[1, slot]
            ).start()
            return carry

        lax.fori_loop(0, cached // BLOCK, fill, 0)

        def store(index, carry, slot=slot, length=length):
            pltpu.make_async_copy(
                new.at[index, slot], full.at[slot, pl.ds(length + index * new_rows, new_rows)], sems.at[1, slot]
            ).start()
            return carry

        lax.fori_loop(0, count, store, 0)
    for slot in range(2):
        whole = full.at[slot, pl.ds(0, cached + fresh)]
        pltpu.make_async_copy(whole, whole, sems.at[1, slot]).wait()
        for block in range(blocks):
            pltpu.make_async_copy(
                full.at[slot, pl.ds(block * BLOCK, BLOCK)],
                out.at[0, table[(2 * group + slot) * blocks + block]],
                sems.at[2, 0],
            ).start()
    pltpu.make_async_copy(out, out, sems.at[2, 0]).wait()


def pages(slot_map, prior_len, table, mixed, new):
    count, _, new_rows, _, width = new.shape
    cached = count * (mixed.shape[1] - 2 * new_rows) // 2
    fresh = count * new_rows
    return pl.pallas_call(
        pages_kernel,
        out_shape=jax.ShapeDtypeStruct((1, 2 * (cached + fresh) // BLOCK, BLOCK, 2, width), BF),
        in_specs=specs("s", "s", "s", "a", "a"),
        out_specs=specs("a")[0],
        scratch_shapes=[
            pltpu.SMEM((count,), jnp.int32),
            pltpu.VMEM((2, 2 * cached + fresh, 2, width), BF),
            pltpu.VMEM((BLOCK, 2, width), BF),
            pltpu.SemaphoreType.DMA((3, 2)),
        ],
        compiler_params=PARAMS,
        name="pages",
    )(slot_map, prior_len, table, mixed, new)


def rotary_tables(prior_count, rows):
    lane = jnp.arange(128, dtype=jnp.int32) % HEAD_DIM
    half_rot = ROTARY // 2
    frequency = ROPE_BASE ** (-2.0 * (lane % half_rot).astype(F32) / ROTARY)
    frequency = jnp.where(lane < ROTARY, frequency, 0.0)
    positions = (prior_count + jnp.arange(rows, dtype=jnp.int32)).astype(F32)
    angles = positions[:, None] * frequency[None, :]
    sine = jnp.sin(angles)
    return (
        jnp.cos(angles),
        jnp.where(lane < half_rot, -sine, 0.0),
        jnp.where((lane >= half_rot) & (lane < ROTARY), sine, 0.0),
    )


def exchange(pieces):
    return lax.all_to_all(pieces, "req", split_axis=0, concat_axis=0, tiled=True)


def layer(
    tokens,
    first_gain,
    first_shift,
    project_weight,
    project_bias,
    output_weight,
    second_gain,
    second_shift,
    expand_weight,
    contract_weight,
    prior_cache,
    prior_len,
    slot_map,
    block_table,
):
    count = slot_map.shape[0]
    rows, width = tokens.shape
    half = rows // 2
    cached = prior_cache.shape[1]
    prior_count = prior_len[lax.axis_index("req")]
    top, bottom = tokens[:half], tokens[half:]
    pieces = ring_gather(top, bottom)
    old = exchange(prior_cache.reshape(count, cached // count, 2, width))
    old_keys, old_values = split(prior_cache[0])
    tables = rotary_tables(prior_count, rows)
    queries, new_keys, new_values = project(
        pieces,
        first_gain.reshape(4, width),
        first_shift.reshape(4, width),
        jnp.transpose(project_weight, (1, 0, 2)),
        project_bias,
        tables,
    )
    parts = attend(prior_len, queries, new_keys, new_values, old_keys, old_values, output_weight)
    mixed = mix(slot_map, old, new_keys, new_values)
    mixed = exchange(mixed)
    top_sum, bottom_sum = ring_scatter(parts)
    top = (top.astype(F32) + top_sum).astype(BF)
    bottom = (bottom.astype(F32) + bottom_sum).astype(BF)
    pieces = ring_gather(top, bottom)
    parts = feed_forward(
        pieces,
        second_gain.reshape(4, width),
        second_shift.reshape(4, width),
        jnp.transpose(expand_weight, (1, 0, 2)),
        contract_weight,
    )
    new = reorder(slot_map, mixed, rows // count)
    new = exchange(new)
    top_sum, bottom_sum = ring_scatter(parts)
    result = jnp.concatenate(
        [(top.astype(F32) + top_sum).astype(BF), (bottom.astype(F32) + bottom_sum).astype(BF)], axis=0
    )
    page_pool = pages(slot_map, prior_len, block_table.reshape(-1), mixed, new)
    return (result, page_pool)


def solution(mesh):
    return jax.shard_map(
        layer,
        mesh=mesh,
        in_specs=(
            P("req", "tp"),
            P(),
            P(),
            P(None, None, "tp"),
            P(None, "tp"),
            P("tp", None),
            P(),
            P(),
            P(None, None, "tp"),
            P("tp", None),
            P("req", None, None, "tp"),
            P(),
            P(),
            P(),
        ),
        out_specs=(P("req", "tp"), P("req", None, None, None, "tp")),
        check_vma=False,
    )
```

```python
import jax
import jax.numpy as jnp
from jax import lax
from jax.experimental import pallas as pl
from jax.experimental.pallas import tpu as pltpu
from jax.sharding import PartitionSpec as P


HEAD_DIM = 64
ROTARY = 16
BLOCK = 256
EPSILON = 1e-05
ROPE_BASE = 10000.0
MASK_FILL = -1e30
BF = jnp.bfloat16
F32 = jnp.float32


OFFSETS = (0, 3, 1, 2)


def shift_by(value, step):
    return lax.ppermute(value, "tp", [(i, (i + step) % 4) for i in range(4)])


def ring_gather(own):
    half = own.shape[0] // 2
    left = shift_by(own, 1)
    right = shift_by(own, -1)
    far_top = shift_by(left[:half], 1)
    far_bottom = shift_by(right[half:], -1)
    return own, left, right, far_top, far_bottom


def add(*terms):
    total = terms[0].astype(F32)
    for term in terms[1:]:
        total = total + term.astype(F32)
    return total


def ring_scatter(base, own, to_right, to_left, right_top, left_bottom):
    half = own.shape[0] // 2
    from_left = shift_by(to_right, 1)
    from_right = shift_by(to_left, -1)
    last_top = shift_by(add(right_top, from_left[:half]).astype(BF), 1)
    last_bottom = shift_by(add(left_bottom, from_right[half:]).astype(BF), -1)
    top = add(own[:half], from_right[:half], last_top)
    bottom = add(own[half:], from_left[half:], last_bottom)
    return (base.astype(F32) + jnp.concatenate([top, bottom], axis=0)).astype(BF)


def store_product(outs, slot, part, half, value):
    own, to_right, to_left, right_top, left_bottom = outs
    place = {
        (0, 0): (own, 0),
        (0, 1): (own, half),
        (1, 0): (to_left, 0),
        (1, 1): (left_bottom, 0),
        (2, 0): (right_top, 0),
        (2, 1): (to_right, half),
        (3, 0): (to_right, 0),
        (3, 1): (to_left, half),
    }
    ref, at = place[slot, part]
    ref[at : at + half, :] = value.astype(BF)


def product_shapes(rows, width):
    whole, half = jax.ShapeDtypeStruct((rows, width), BF), jax.ShapeDtypeStruct((rows // 2, width), BF)
    return (whole, whole, whole, half, half)


def norm_into(normed, pieces, gain, shift, blocks, half):
    width = pieces[0].shape[1]
    total = 4 * width
    step = 64
    for part in range(2):
        own, left, right, far_top, far_bottom = pieces
        refs = [ref.at[part * half : (part + 1) * half] for ref in (own, left, right)]
        refs.append((far_top, far_bottom)[part])

        def body(index, carry, refs=refs, part=part):
            at = pl.multiple_of(index * step, step)
            rows = [ref[pl.ds(at, step), :].astype(F32) for ref in refs]
            mean = sum(jnp.sum(row, axis=1, keepdims=True) for row in rows) / total
            rows = [row - mean for row in rows]
            spread = sum(jnp.sum(row * row, axis=1, keepdims=True) for row in rows) / total
            scale = lax.rsqrt(spread + EPSILON)
            for slot, row in enumerate(rows):
                line = blocks[slot]
                value = row * scale * gain[pl.ds(line, 1), :] + shift[pl.ds(line, 1), :]
                normed[pl.ds(part * half + at, step), slot * width : (slot + 1) * width] = value.astype(BF)
            return carry

        lax.fori_loop(0, half // step, body, 0)


def project_kernel(
    own, left, right, far_top, far_bottom, gain, shift, weight, bias, cosine, sine_a, sine_b, queries, keys, values, buffer, normed, sems
):
    device = lax.axis_index("tp")
    half, width = far_top.shape
    blocks = [lax.rem(device + offset, 4) for offset in OFFSETS]
    copies = []
    for slot in range(4):
        copies.append(
            pltpu.make_async_copy(
                weight.at[:, pl.ds(blocks[slot] * width, width), :],
                buffer.at[:, pl.ds(slot * width, width), :],
                sems.at[slot],
            )
        )
        copies[-1].start()
    norm_into(normed, (own, left, right, far_top, far_bottom), gain, shift, blocks, half)
    for copy in copies:
        copy.wait()
    outs = (queries, keys, values)
    for part in range(2):
        rows = slice(part * half, (part + 1) * half)
        for which in range(3):
            product = jnp.dot(normed[rows, :], buffer[which], preferred_element_type=F32)
            product = product + bias[which : which + 1, :]
            if which == 2:
                outs[which][rows, :] = product.astype(BF)
                continue
            for tile in range(width // 128):
                lanes = slice(tile * 128, (tile + 1) * 128)
                value = product[:, lanes]
                up = pltpu.roll(value, 128 - ROTARY // 2, 1)
                down = pltpu.roll(value, ROTARY // 2, 1)
                turned = value * cosine[rows, :] + up * sine_a[rows, :] + down * sine_b[rows, :]
                if which == 0:
                    turned = turned * HEAD_DIM ** (-0.5)
                outs[which][rows, lanes] = turned.astype(BF)


VMEM = pltpu.MemorySpace.VMEM
SMEM = pltpu.MemorySpace.SMEM


def specs(*kinds):
    table = {"v": pl.BlockSpec(memory_space=VMEM), "s": pl.BlockSpec(memory_space=SMEM), "a": pl.BlockSpec(memory_space=pltpu.MemorySpace.HBM)}
    return [table[kind] for kind in kinds]


PARAMS = pltpu.CompilerParams(vmem_limit_bytes=56 * 1024 * 1024)


def project(pieces, gain, shift, weight, bias, tables):
    half, width = pieces[-1].shape
    out = jax.ShapeDtypeStruct((2 * half, width), BF)
    return pl.pallas_call(
        project_kernel,
        out_shape=(out, out, out),
        in_specs=specs(*"v" * 5, "v", "v", "a", "v", "v", "v", "v"),
        out_specs=tuple(specs("v", "v", "v")),
        scratch_shapes=[
            pltpu.VMEM((3, 4 * width, width), BF),
            pltpu.VMEM((2 * half, 4 * width), BF),
            pltpu.SemaphoreType.DMA((4,)),
        ],
        compiler_params=PARAMS,
        name="project",
    )(*pieces, gain, shift, weight, bias, *tables)


def attend_kernel(lengths, queries, new_keys, new_values, old_keys, old_values, weight, *refs):
    outs, (buffer, mixed, sems) = refs[:5], refs[5:]
    device = lax.axis_index("tp")
    prior = lengths[lax.axis_index("req")]
    rows_all, width = queries.shape
    cached = old_keys.shape[0]
    blocks = [lax.rem(device + offset, 4) for offset in OFFSETS]
    copies = []
    for slot in range(4):
        copies.append(
            pltpu.make_async_copy(
                weight.at[:, pl.ds(blocks[slot] * width, width)], buffer.at[:, slot * width : (slot + 1) * width], sems.at[slot]
            )
        )
        copies[-1].start()
    step = 256
    contract = (((1,), (1,)), ((), ()))
    for part in range(rows_all // step):
        rows = slice(part * step, (part + 1) * step)
        seen = (part + 1) * step

        def body(pair, carry, rows=rows, seen=seen, part=part):
            lanes = pl.ds(pl.multiple_of(pair * 128, 128), 128)
            query = queries[rows, lanes]
            old_key, new_key = old_keys[:, lanes], new_keys[:seen, lanes]
            old_value, new_value = old_values[:, lanes], new_values[:seen, lanes]
            lane = lax.broadcasted_iota(jnp.int32, (step, 128), 1)
            old_allowed = lax.broadcasted_iota(jnp.int32, (1, cached), 1) < prior
            new_allowed = lax.broadcasted_iota(jnp.int32, (step, seen), 1) <= lax.broadcasted_iota(
                jnp.int32, (step, seen), 0
            ) + part * step
            results = []
            for head in range(2):
                own = (lane < HEAD_DIM) if head == 0 else (lane >= HEAD_DIM)
                masked = jnp.where(own, query, jnp.zeros((), BF))
                old_score = lax.dot_general(masked, old_key, contract, preferred_element_type=F32)
                old_score = jnp.where(old_allowed, old_score, MASK_FILL)
                new_score = lax.dot_general(masked, new_key, contract, preferred_element_type=F32)
                new_score = jnp.where(new_allowed, new_score, MASK_FILL)
                highest = jnp.maximum(
                    jnp.max(old_score, axis=1, keepdims=True), jnp.max(new_score, axis=1, keepdims=True)
                )
                old_weight = jnp.exp(old_score - highest)
                new_weight = jnp.exp(new_score - highest)
                total = jnp.sum(old_weight, axis=1, keepdims=True) + jnp.sum(new_weight, axis=1, keepdims=True)
                value = jnp.dot(old_weight.astype(BF), old_value, preferred_element_type=F32) + jnp.dot(
                    new_weight.astype(BF), new_value, preferred_element_type=F32
                )
                results.append(value / total)
            mixed[rows, lanes] = jnp.where(lane < HEAD_DIM, results[0], results[1]).astype(BF)
            return carry

        lax.fori_loop(0, width // 128, body, 0)
    for copy in copies:
        copy.wait()
    for part in range(rows_all // step):
        rows = slice(part * step, (part + 1) * step)
        for slot in range(4):
            product = jnp.dot(mixed[rows, :], buffer[:, slot * width : (slot + 1) * width], preferred_element_type=F32)
            store_product(outs, slot, part, step, product)


def attend(lengths, queries, new_keys, new_values, old_keys, old_values, weight):
    rows, width = queries.shape
    return pl.pallas_call(
        attend_kernel,
        out_shape=product_shapes(rows, width),
        in_specs=specs("s", "v", "v", "v", "v", "v", "a"),
        out_specs=tuple(specs(*"v" * 5)),
        scratch_shapes=[pltpu.VMEM((width, 4 * width), BF), pltpu.VMEM((rows, width), BF), pltpu.SemaphoreType.DMA((4,))],
        compiler_params=PARAMS,
        name="attend",
    )(lengths, queries, new_keys, new_values, old_keys, old_values, weight)


def forward_kernel(own, left, right, far_top, far_bottom, gain, shift, expand, contract, *refs):
    outs, (expand_buffer, contract_buffer, normed, sems) = refs[:5], refs[5:]
    device = lax.axis_index("tp")
    half, width = far_top.shape
    blocks = [lax.rem(device + offset, 4) for offset in OFFSETS]
    copies = []
    for slot in range(4):
        copies.append(
            pltpu.make_async_copy(
                expand.at[:, pl.ds(blocks[slot] * width, width), :],
                expand_buffer.at[:, slot * width : (slot + 1) * width, :],
                sems.at[0, slot],
            )
        )
    for slot in range(4):
        copies.append(
            pltpu.make_async_copy(
                contract.at[:, pl.ds(blocks[slot] * width, width)],
                contract_buffer.at[:, slot * width : (slot + 1) * width],
                sems.at[1, slot],
            )
        )
    for copy in copies:
        copy.start()
    norm_into(normed, (own, left, right, far_top, far_bottom), gain, shift, blocks, half)
    for copy in copies:
        copy.wait()
    for part in range(2):
        rows = slice(part * half, (part + 1) * half)
        gate = jnp.dot(normed[rows, :], expand_buffer[0], preferred_element_type=F32)
        up = jnp.dot(normed[rows, :], expand_buffer[1], preferred_element_type=F32)
        hidden = (gate / (1.0 + jnp.exp(-gate)) * up).astype(BF)
        for slot in range(4):
            product = jnp.dot(hidden, contract_buffer[:, slot * width : (slot + 1) * width], preferred_element_type=F32)
            store_product(outs, slot, part, half, product)


def feed_forward(pieces, gain, shift, expand, contract):
    half, width = pieces[-1].shape
    hidden = expand.shape[2]
    return pl.pallas_call(
        forward_kernel,
        out_shape=product_shapes(2 * half, width),
        in_specs=specs(*"v" * 5, "v", "v", "a", "a"),
        out_specs=tuple(specs(*"v" * 5)),
        scratch_shapes=[
            pltpu.VMEM((2, 4 * width, hidden), BF),
            pltpu.VMEM((hidden, 4 * width), BF),
            pltpu.VMEM((2 * half, 4 * width), BF),
            pltpu.SemaphoreType.DMA((2, 4)),
        ],
        compiler_params=PARAMS,
        name="feed_forward",
    )(*pieces, gain, shift, expand, contract)


def split_kernel(cache, keys, values):
    _, _, width = cache.shape
    step = 128
    row = lax.broadcasted_iota(jnp.int32, (2 * step, 2 * step), 0)
    column = lax.broadcasted_iota(jnp.int32, (2 * step, 2 * step), 1)
    source = jnp.where(row < step, 2 * row, 2 * (row - step) + 1)
    chosen = jnp.where(column == source, 1.0, 0.0).astype(BF)

    def body(index, carry):
        at = pl.multiple_of(index * step, step)
        pair = cache[pl.ds(at, step)].reshape(2 * step, width)
        parted = jnp.dot(chosen, pair, preferred_element_type=F32).astype(BF)
        keys[pl.ds(at, step), :] = parted[:step]
        values[pl.ds(at, step), :] = parted[step:]
        return carry

    lax.fori_loop(0, cache.shape[0] // step, body, 0)


def split(cache):
    rows, _, width = cache.shape
    out = jax.ShapeDtypeStruct((rows, width), BF)
    return pl.pallas_call(
        split_kernel,
        out_shape=(out, out),
        in_specs=specs("v"),
        out_specs=tuple(specs("v", "v")),
        compiler_params=PARAMS,
        name="split",
    )(cache)


def find_owners(slot_map, owners):
    def body(index, carry):
        owners[slot_map[index]] = index
        return carry

    lax.fori_loop(0, slot_map.shape[0], body, 0)


def mix_kernel(slot_map, pieces, keys, values, out, owners, stage, sems):
    count, rows, _, width = pieces.shape
    half = width // 2
    fresh = keys.shape[0] // count
    find_owners(slot_map, owners)

    def send(slot, carry):
        group = slot // 2
        for side in range(2):
            pltpu.make_async_copy(
                pieces.at[owners[slot], :, :, side * half : (side + 1) * half],
                out.at[2 * group + side, pl.ds((slot - 2 * group) * rows, rows)],
                sems.at[0],
            ).start()
        return carry

    lax.fori_loop(0, count, send, 0)

    def weave(slot, carry):
        at = pl.multiple_of(slot * fresh, fresh)
        for side in range(2):
            lanes = slice(side * half, (side + 1) * half)
            stage[slot, side * fresh : (side + 1) * fresh, 0, :] = keys[pl.ds(at, fresh), lanes]
            stage[slot, side * fresh : (side + 1) * fresh, 1, :] = values[pl.ds(at, fresh), lanes]
        return carry

    lax.fori_loop(0, count, weave, 0)
    last = pltpu.make_async_copy(stage, out.at[:, 2 * rows :], sems.at[1])
    last.start()
    first = out.at[:, : 2 * rows]
    pltpu.make_async_copy(first, first, sems.at[0]).wait()
    last.wait()


def mix(slot_map, pieces, keys, values):
    count, rows, _, width = pieces.shape
    fresh = keys.shape[0] // count
    return pl.pallas_call(
        mix_kernel,
        out_shape=jax.ShapeDtypeStruct((count, 2 * rows + 2 * fresh, 2, width // 2), BF),
        in_specs=specs("s", "v", "v", "v"),
        out_specs=specs("a")[0],
        scratch_shapes=[
            pltpu.SMEM((count,), jnp.int32),
            pltpu.VMEM((count, 2 * fresh, 2, width // 2), BF),
            pltpu.SemaphoreType.DMA((2,)),
        ],
        compiler_params=PARAMS,
        name="mix",
    )(slot_map, pieces, keys, values)


def reorder_kernel(slot_map, mixed, out, owners, sem):
    count, rows, _, _ = mixed.shape
    fresh = out.shape[2]
    find_owners(slot_map, owners)

    def send(slot, carry):
        group = slot // 2
        for side in range(2):
            pltpu.make_async_copy(
                mixed.at[owners[slot], pl.ds(rows - (2 - side) * fresh, fresh)],
                out.at[2 * group + side, slot - 2 * group],
                sem,
            ).start()
        return carry

    lax.fori_loop(0, count, send, 0)
    pltpu.make_async_copy(out, out, sem).wait()


def reorder(slot_map, mixed, fresh):
    count, _, _, width = mixed.shape
    return pl.pallas_call(
        reorder_kernel,
        out_shape=jax.ShapeDtypeStruct((count, 2, fresh, 2, width), BF),
        in_specs=specs("s", "a"),
        out_specs=specs("v")[0],
        scratch_shapes=[pltpu.SMEM((count,), jnp.int32), pltpu.SemaphoreType.DMA],
        compiler_params=PARAMS,
        name="reorder",
    )(slot_map, mixed)


def pages_kernel(slot_map, prior_len, table, mixed, new, out, owners, full, blank, sems):
    count, _, new_rows, _, _ = new.shape
    old_rows = (mixed.shape[1] - 2 * new_rows) // 2
    cached, fresh = count * old_rows, count * new_rows
    blocks = (cached + fresh) // BLOCK
    group = lax.axis_index("req") // 2
    find_owners(slot_map, owners)
    for slot in range(2):

        def load(index, carry, slot=slot):
            pltpu.make_async_copy(
                mixed.at[index, pl.ds(slot * old_rows, old_rows)], full.at[slot, pl.ds(index * old_rows, old_rows)], sems.at[0, slot]
            ).start()
            return carry

        lax.fori_loop(0, count, load, 0)
    blank[...] = jnp.zeros(blank.shape, BF)
    for slot in range(2):
        whole = full.at[slot, pl.ds(0, cached)]
        pltpu.make_async_copy(whole, whole, sems.at[0, slot]).wait()
        length = prior_len[owners[2 * group + slot]]

        def fill(index, carry, slot=slot, length=length):
            pltpu.make_async_copy(
                blank, full.at[slot, pl.ds(length + fresh + index * BLOCK, BLOCK)], sems.at[1, slot]
            ).start()
            return carry

        lax.fori_loop(0, cached // BLOCK, fill, 0)

        def store(index, carry, slot=slot, length=length):
            pltpu.make_async_copy(
                new.at[index, slot], full.at[slot, pl.ds(length + index * new_rows, new_rows)], sems.at[1, slot]
            ).start()
            return carry

        lax.fori_loop(0, count, store, 0)
    for slot in range(2):
        whole = full.at[slot, pl.ds(0, cached + fresh)]
        pltpu.make_async_copy(whole, whole, sems.at[1, slot]).wait()
        for block in range(blocks):
            pltpu.make_async_copy(
                full.at[slot, pl.ds(block * BLOCK, BLOCK)],
                out.at[0, table[(2 * group + slot) * blocks + block]],
                sems.at[2, 0],
            ).start()
    pltpu.make_async_copy(out, out, sems.at[2, 0]).wait()


def pages(slot_map, prior_len, table, mixed, new):
    count, _, new_rows, _, width = new.shape
    cached = count * (mixed.shape[1] - 2 * new_rows) // 2
    fresh = count * new_rows
    return pl.pallas_call(
        pages_kernel,
        out_shape=jax.ShapeDtypeStruct((1, 2 * (cached + fresh) // BLOCK, BLOCK, 2, width), BF),
        in_specs=specs("s", "s", "s", "a", "a"),
        out_specs=specs("a")[0],
        scratch_shapes=[
            pltpu.SMEM((count,), jnp.int32),
            pltpu.VMEM((2, 2 * cached + fresh, 2, width), BF),
            pltpu.VMEM((BLOCK, 2, width), BF),
            pltpu.SemaphoreType.DMA((3, 2)),
        ],
        compiler_params=PARAMS,
        name="pages",
    )(slot_map, prior_len, table, mixed, new)


def rotary_tables(prior_count, rows):
    lane = jnp.arange(128, dtype=jnp.int32) % HEAD_DIM
    half_rot = ROTARY // 2
    frequency = ROPE_BASE ** (-2.0 * (lane % half_rot).astype(F32) / ROTARY)
    frequency = jnp.where(lane < ROTARY, frequency, 0.0)
    positions = (prior_count + jnp.arange(rows, dtype=jnp.int32)).astype(F32)
    angles = positions[:, None] * frequency[None, :]
    sine = jnp.sin(angles)
    return (
        jnp.cos(angles),
        jnp.where(lane < half_rot, -sine, 0.0),
        jnp.where((lane >= half_rot) & (lane < ROTARY), sine, 0.0),
    )


def exchange(pieces):
    return lax.all_to_all(pieces, "req", split_axis=0, concat_axis=0, tiled=True)


def layer(
    tokens,
    first_gain,
    first_shift,
    project_weight,
    project_bias,
    output_weight,
    second_gain,
    second_shift,
    expand_weight,
    contract_weight,
    prior_cache,
    prior_len,
    slot_map,
    block_table,
):
    count = slot_map.shape[0]
    rows, width = tokens.shape
    cached = prior_cache.shape[1]
    prior_count = prior_len[lax.axis_index("req")]
    pieces = ring_gather(tokens)
    old = exchange(prior_cache.reshape(count, cached // count, 2, width))
    old_keys, old_values = split(prior_cache[0])
    tables = rotary_tables(prior_count, rows)
    queries, new_keys, new_values = project(
        pieces,
        first_gain.reshape(4, width),
        first_shift.reshape(4, width),
        jnp.transpose(project_weight, (1, 0, 2)),
        project_bias,
        tables,
    )
    mixed = mix(slot_map, old, new_keys, new_values)
    mixed = exchange(mixed)
    parts = attend(prior_len, queries, new_keys, new_values, old_keys, old_values, output_weight)
    residual = ring_scatter(tokens, *parts)
    expand = jnp.transpose(expand_weight, (1, 0, 2))
    residual, expand = lax.optimization_barrier((residual, expand))
    pieces = ring_gather(residual)
    parts = feed_forward(pieces, second_gain.reshape(4, width), second_shift.reshape(4, width), expand, contract_weight)
    new = reorder(slot_map, mixed, rows // count)
    new = exchange(new)
    result = ring_scatter(residual, *parts)
    page_pool = pages(slot_map, prior_len, block_table.reshape(-1), mixed, new)
    return (result, page_pool)


def solution(mesh):
    return jax.shard_map(
        layer,
        mesh=mesh,
        in_specs=(
            P("req", "tp"),
            P(),
            P(),
            P(None, None, "tp"),
            P(None, "tp"),
            P("tp", None),
            P(),
            P(),
            P(None, None, "tp"),
            P("tp", None),
            P("req", None, None, "tp"),
            P(),
            P(),
            P(),
        ),
        out_specs=(P("req", "tp"), P("req", None, None, None, "tp")),
        check_vma=False,
    )
```

```python
import jax
import jax.numpy as jnp
from jax import lax
from jax.experimental import pallas as pl
from jax.experimental.pallas import tpu as pltpu
from jax.sharding import PartitionSpec as P


HEAD_DIM = 64
ROTARY = 16
BLOCK = 256
EPSILON = 1e-05
ROPE_BASE = 10000.0
MASK_FILL = -1e30
BF = jnp.bfloat16
F32 = jnp.float32


OFFSETS = (0, 3, 1, 2)
EARLY = 8


def shift_by(value, step):
    return lax.ppermute(value, "tp", [(i, (i + step) % 4) for i in range(4)])


def ring_gather(top, bottom):
    left_top = shift_by(top, 1)
    right_bottom = shift_by(bottom, -1)
    left_bottom = shift_by(bottom, 1)
    right_top = shift_by(top, -1)
    far_top = shift_by(left_top, 1)
    far_bottom = shift_by(right_bottom, -1)
    return (top, bottom, left_top, left_bottom, right_top, right_bottom, far_top, far_bottom)


def ring_scatter(parts):
    own_top, own_bottom, left_top, left_bottom, right_top, right_bottom, far_top, far_bottom = parts
    add = lambda a, b: (a.astype(F32) + b.astype(F32))
    far_top = shift_by(far_top, 1)
    far_bottom = shift_by(far_bottom, -1)
    from_left_bottom = shift_by(right_bottom, 1)
    from_right_top = shift_by(left_top, -1)
    from_left_top = shift_by(add(right_top, far_top).astype(BF), 1)
    from_right_bottom = shift_by(add(left_bottom, far_bottom).astype(BF), -1)
    top = add(own_top, from_right_top) + from_left_top.astype(F32)
    bottom = add(own_bottom, from_left_bottom) + from_right_bottom.astype(F32)
    return top, bottom


def norm_into(normed, pieces, gain, shift, blocks, half):
    width = pieces[0].shape[1]
    total = 4 * width
    step = 64
    for part in range(2):
        refs = pieces[part::2]

        def body(index, carry, refs=refs, part=part):
            at = pl.multiple_of(index * step, step)
            rows = [ref[pl.ds(at, step), :].astype(F32) for ref in refs]
            mean = sum(jnp.sum(row, axis=1, keepdims=True) for row in rows) / total
            rows = [row - mean for row in rows]
            spread = sum(jnp.sum(row * row, axis=1, keepdims=True) for row in rows) / total
            scale = lax.rsqrt(spread + EPSILON)
            for slot, row in enumerate(rows):
                line = blocks[slot]
                value = row * scale * gain[pl.ds(line, 1), :] + shift[pl.ds(line, 1), :]
                normed[pl.ds(part * half + at, step), slot * width : (slot + 1) * width] = value.astype(BF)
            return carry

        lax.fori_loop(0, half // step, body, 0)


def project_kernel(
    o0, o1, l0, l1, r0, r1, f0, f1, gain, shift, weight, bias, cosine, sine_a, sine_b, queries, keys, values, buffer, normed, sems
):
    device = lax.axis_index("tp")
    width = o0.shape[1]
    half = o0.shape[0]
    blocks = [lax.rem(device + offset, 4) for offset in OFFSETS]
    copies = []
    for slot in range(4):
        copies.append(
            pltpu.make_async_copy(
                weight.at[:, pl.ds(blocks[slot] * width, width), :],
                buffer.at[:, pl.ds(slot * width, width), :],
                sems.at[slot],
            )
        )
        copies[-1].start()
    norm_into(normed, (o0, o1, l0, l1, r0, r1, f0, f1), gain, shift, blocks, half)
    for copy in copies:
        copy.wait()
    outs = (queries, keys, values)
    for part in range(2):
        rows = slice(part * half, (part + 1) * half)
        for which in range(3):
            product = jnp.dot(normed[rows, :], buffer[which], preferred_element_type=F32)
            product = product + bias[which : which + 1, :]
            if which == 2:
                outs[which][rows, :] = product.astype(BF)
                continue
            for tile in range(width // 128):
                lanes = slice(tile * 128, (tile + 1) * 128)
                value = product[:, lanes]
                up = pltpu.roll(value, 128 - ROTARY // 2, 1)
                down = pltpu.roll(value, ROTARY // 2, 1)
                turned = value * cosine[rows, :] + up * sine_a[rows, :] + down * sine_b[rows, :]
                if which == 0:
                    turned = turned * HEAD_DIM ** (-0.5)
                outs[which][rows, lanes] = turned.astype(BF)


VMEM = pltpu.MemorySpace.VMEM
SMEM = pltpu.MemorySpace.SMEM


def specs(*kinds):
    table = {"v": pl.BlockSpec(memory_space=VMEM), "s": pl.BlockSpec(memory_space=SMEM), "a": pl.BlockSpec(memory_space=pl.ANY)}
    return [table[kind] for kind in kinds]


PARAMS = pltpu.CompilerParams(vmem_limit_bytes=56 * 1024 * 1024)


def project(pieces, gain, shift, weight, bias, tables):
    half, width = pieces[0].shape
    out = jax.ShapeDtypeStruct((2 * half, width), BF)
    return pl.pallas_call(
        project_kernel,
        out_shape=(out, out, out),
        in_specs=specs(*"v" * 8, "v", "v", "a", "v", "v", "v", "v"),
        out_specs=tuple(specs("v", "v", "v")),
        scratch_shapes=[
            pltpu.VMEM((3, 4 * width, width), BF),
            pltpu.VMEM((2 * half, 4 * width), BF),
            pltpu.SemaphoreType.DMA((4,)),
        ],
        compiler_params=PARAMS,
        name="project",
    )(*pieces, gain, shift, weight, bias, *tables)


def attend_kernel(lengths, queries, new_keys, new_values, old_keys, old_values, weight, *refs):
    outs, (buffer, mixed, sems) = refs[:8], refs[8:]
    device = lax.axis_index("tp")
    prior = lengths[lax.axis_index("req")]
    rows_all, width = queries.shape
    cached = old_keys.shape[0]
    blocks = [lax.rem(device + offset, 4) for offset in OFFSETS]
    copies = []
    for slot in range(4):
        copies.append(
            pltpu.make_async_copy(
                weight.at[:, pl.ds(blocks[slot] * width, width)], buffer.at[:, slot * width : (slot + 1) * width], sems.at[slot]
            )
        )
        copies[-1].start()
    step = 256
    contract = (((1,), (1,)), ((), ()))
    for part in range(rows_all // step):
        rows = slice(part * step, (part + 1) * step)
        seen = (part + 1) * step

        def body(pair, carry, rows=rows, seen=seen, part=part):
            lanes = pl.ds(pl.multiple_of(pair * 128, 128), 128)
            query = queries[rows, lanes]
            old_key, new_key = old_keys[:, lanes], new_keys[:seen, lanes]
            old_value, new_value = old_values[:, lanes], new_values[:seen, lanes]
            lane = lax.broadcasted_iota(jnp.int32, (step, 128), 1)
            old_allowed = lax.broadcasted_iota(jnp.int32, (1, cached), 1) < prior
            new_allowed = lax.broadcasted_iota(jnp.int32, (step, seen), 1) <= lax.broadcasted_iota(
                jnp.int32, (step, seen), 0
            ) + part * step
            results = []
            for head in range(2):
                own = (lane < HEAD_DIM) if head == 0 else (lane >= HEAD_DIM)
                masked = jnp.where(own, query, jnp.zeros((), BF))
                old_score = lax.dot_general(masked, old_key, contract, preferred_element_type=F32)
                old_score = jnp.where(old_allowed, old_score, MASK_FILL)
                new_score = lax.dot_general(masked, new_key, contract, preferred_element_type=F32)
                new_score = jnp.where(new_allowed, new_score, MASK_FILL)
                highest = jnp.maximum(
                    jnp.max(old_score, axis=1, keepdims=True), jnp.max(new_score, axis=1, keepdims=True)
                )
                old_weight = jnp.exp(old_score - highest)
                new_weight = jnp.exp(new_score - highest)
                total = jnp.sum(old_weight, axis=1, keepdims=True) + jnp.sum(new_weight, axis=1, keepdims=True)
                value = jnp.dot(old_weight.astype(BF), old_value, preferred_element_type=F32) + jnp.dot(
                    new_weight.astype(BF), new_value, preferred_element_type=F32
                )
                results.append(value / total)
            mixed[rows, lanes] = jnp.where(lane < HEAD_DIM, results[0], results[1]).astype(BF)
            return carry

        lax.fori_loop(0, width // 128, body, 0)
    for copy in copies:
        copy.wait()
    for part in range(rows_all // step):
        rows = slice(part * step, (part + 1) * step)
        for slot in range(4):
            product = jnp.dot(mixed[rows, :], buffer[:, slot * width : (slot + 1) * width], preferred_element_type=F32)
            outs[2 * slot + part][...] = product.astype(BF)


def attend(lengths, queries, new_keys, new_values, old_keys, old_values, weight):
    rows, width = queries.shape
    return pl.pallas_call(
        attend_kernel,
        out_shape=(jax.ShapeDtypeStruct((rows // 2, width), BF),) * 8,
        in_specs=specs("s", "v", "v", "v", "v", "v", "a"),
        out_specs=tuple(specs(*"v" * 8)),
        scratch_shapes=[pltpu.VMEM((width, 4 * width), BF), pltpu.VMEM((rows, width), BF), pltpu.SemaphoreType.DMA((4,))],
        compiler_params=PARAMS,
        name="attend",
    )(lengths, queries, new_keys, new_values, old_keys, old_values, weight)


def forward_kernel(o0, o1, l0, l1, r0, r1, f0, f1, gain, shift, expand, contract, *refs):
    outs, (expand_buffer, contract_buffer, normed, sems) = refs[:8], refs[8:]
    device = lax.axis_index("tp")
    half, width = o0.shape
    blocks = [lax.rem(device + offset, 4) for offset in OFFSETS]
    copies = []
    for slot in range(4):
        copies.append(
            pltpu.make_async_copy(
                expand.at[:, pl.ds(blocks[slot] * width, width), :],
                expand_buffer.at[:, slot * width : (slot + 1) * width, :],
                sems.at[0, slot],
            )
        )
    for slot in range(4):
        copies.append(
            pltpu.make_async_copy(
                contract.at[:, pl.ds(blocks[slot] * width, width)],
                contract_buffer.at[:, slot * width : (slot + 1) * width],
                sems.at[1, slot],
            )
        )
    for copy in copies:
        copy.start()
    norm_into(normed, (o0, o1, l0, l1, r0, r1, f0, f1), gain, shift, blocks, half)
    for copy in copies:
        copy.wait()
    for part in range(2):
        rows = slice(part * half, (part + 1) * half)
        gate = jnp.dot(normed[rows, :], expand_buffer[0], preferred_element_type=F32)
        up = jnp.dot(normed[rows, :], expand_buffer[1], preferred_element_type=F32)
        hidden = (gate / (1.0 + jnp.exp(-gate)) * up).astype(BF)
        for slot in range(4):
            product = jnp.dot(hidden, contract_buffer[:, slot * width : (slot + 1) * width], preferred_element_type=F32)
            outs[2 * slot + part][...] = product.astype(BF)


def feed_forward(pieces, gain, shift, expand, contract):
    half, width = pieces[0].shape
    hidden = expand.shape[2]
    return pl.pallas_call(
        forward_kernel,
        out_shape=(jax.ShapeDtypeStruct((half, width), BF),) * 8,
        in_specs=specs(*"v" * 8, "v", "v", "a", "a"),
        out_specs=tuple(specs(*"v" * 8)),
        scratch_shapes=[
            pltpu.VMEM((2, 4 * width, hidden), BF),
            pltpu.VMEM((hidden, 4 * width), BF),
            pltpu.VMEM((2 * half, 4 * width), BF),
            pltpu.SemaphoreType.DMA((2, 4)),
        ],
        compiler_params=PARAMS,
        name="feed_forward",
    )(*pieces, gain, shift, expand, contract)


def split_kernel(cache, keys, values):
    _, _, width = cache.shape
    step = 128
    row = lax.broadcasted_iota(jnp.int32, (2 * step, 2 * step), 0)
    column = lax.broadcasted_iota(jnp.int32, (2 * step, 2 * step), 1)
    source = jnp.where(row < step, 2 * row, 2 * (row - step) + 1)
    chosen = jnp.where(column == source, 1.0, 0.0).astype(BF)

    def body(index, carry):
        at = pl.multiple_of(index * step, step)
        pair = cache[pl.ds(at, step)].reshape(2 * step, width)
        parted = jnp.dot(chosen, pair, preferred_element_type=F32).astype(BF)
        keys[pl.ds(at, step), :] = parted[:step]
        values[pl.ds(at, step), :] = parted[step:]
        return carry

    lax.fori_loop(0, cache.shape[0] // step, body, 0)


def split(cache):
    rows, _, width = cache.shape
    out = jax.ShapeDtypeStruct((rows, width), BF)
    return pl.pallas_call(
        split_kernel,
        out_shape=(out, out),
        in_specs=specs("v"),
        out_specs=tuple(specs("v", "v")),
        compiler_params=PARAMS,
        name="split",
    )(cache)


def find_owners(slot_map, owners):
    def body(index, carry):
        owners[slot_map[index]] = index
        return carry

    lax.fori_loop(0, slot_map.shape[0], body, 0)


def send_old(pieces, owners, out, sem, first, rows):
    half = pieces.shape[3] // 2

    def send(slot, carry):
        group = slot // 2
        for side in range(2):
            pltpu.make_async_copy(
                pieces.at[owners[slot], pl.ds(first, rows), :, side * half : (side + 1) * half],
                out.at[2 * group + side, pl.ds((slot - 2 * group) * rows, rows)],
                sem,
            ).start()
        return carry

    lax.fori_loop(0, pieces.shape[0], send, 0)


def mix_kernel(slot_map, pieces, keys, values, out, owners, stage, sems):
    count = pieces.shape[0]
    half = pieces.shape[3] // 2
    fresh = keys.shape[0] // count
    early = out.shape[1] // 2 - fresh
    find_owners(slot_map, owners)
    send_old(pieces, owners, out, sems.at[0], 0, early)

    def weave(slot, carry):
        at = pl.multiple_of(slot * fresh, fresh)
        for side in range(2):
            lanes = slice(side * half, (side + 1) * half)
            stage[slot, side * fresh : (side + 1) * fresh, 0, :] = keys[pl.ds(at, fresh), lanes]
            stage[slot, side * fresh : (side + 1) * fresh, 1, :] = values[pl.ds(at, fresh), lanes]
        return carry

    lax.fori_loop(0, count, weave, 0)
    last = pltpu.make_async_copy(stage, out.at[:, 2 * early :], sems.at[1])
    last.start()
    first = out.at[:, : 2 * early]
    pltpu.make_async_copy(first, first, sems.at[0]).wait()
    last.wait()


def mix(slot_map, pieces, keys, values, early):
    count, _, _, width = pieces.shape
    fresh = keys.shape[0] // count
    return pl.pallas_call(
        mix_kernel,
        out_shape=jax.ShapeDtypeStruct((count, 2 * early + 2 * fresh, 2, width // 2), BF),
        in_specs=specs("s", "v", "v", "v"),
        out_specs=specs("a")[0],
        scratch_shapes=[
            pltpu.SMEM((count,), jnp.int32),
            pltpu.VMEM((count, 2 * fresh, 2, width // 2), BF),
            pltpu.SemaphoreType.DMA((2,)),
        ],
        compiler_params=PARAMS,
        name="mix",
    )(slot_map, pieces, keys, values)


def reorder_kernel(slot_map, pieces, mixed, out, owners, stage, sems):
    count, rows, _, _ = pieces.shape
    fresh = stage.shape[1] // 2
    late = out.shape[1] // 2 - fresh
    early = rows - late
    find_owners(slot_map, owners)

    def load(slot, carry):
        pltpu.make_async_copy(mixed.at[owners[slot], pl.ds(2 * early, 2 * fresh)], stage.at[slot], sems.at[0]).start()
        return carry

    lax.fori_loop(0, count, load, 0)
    send_old(pieces, owners, out, sems.at[1], early, late)
    pltpu.make_async_copy(stage, stage, sems.at[0]).wait()

    def send(slot, carry):
        group = slot // 2
        for side in range(2):
            pltpu.make_async_copy(
                stage.at[slot, pl.ds(side * fresh, fresh)],
                out.at[2 * group + side, pl.ds(2 * late + (slot - 2 * group) * fresh, fresh)],
                sems.at[2],
            ).start()
        return carry

    lax.fori_loop(0, count, send, 0)
    first, last = out.at[:, : 2 * late], out.at[:, 2 * late :]
    pltpu.make_async_copy(first, first, sems.at[1]).wait()
    pltpu.make_async_copy(last, last, sems.at[2]).wait()


def reorder(slot_map, pieces, mixed, fresh):
    count, rows, _, width = pieces.shape
    late = rows - (mixed.shape[1] // 2 - fresh)
    return pl.pallas_call(
        reorder_kernel,
        out_shape=jax.ShapeDtypeStruct((count, 2 * late + 2 * fresh, 2, width // 2), BF),
        in_specs=specs("s", "v", "a"),
        out_specs=specs("a")[0],
        scratch_shapes=[
            pltpu.SMEM((count,), jnp.int32),
            pltpu.VMEM((count, 2 * fresh, 2, width // 2), BF),
            pltpu.SemaphoreType.DMA((3,)),
        ],
        compiler_params=PARAMS,
        name="reorder",
    )(slot_map, pieces, mixed)


def pages_kernel(slot_map, prior_len, table, mixed, rest, out, owners, full, blank, sems):
    count = mixed.shape[0]
    blocks = out.shape[1] // 2
    new_rows = (mixed.shape[1] + rest.shape[1]) // 2 - blocks * BLOCK // count
    early = mixed.shape[1] // 2 - new_rows
    late = rest.shape[1] // 2 - new_rows
    old_rows = early + late
    cached, fresh = count * old_rows, count * new_rows
    group = lax.axis_index("req") // 2
    find_owners(slot_map, owners)
    for slot in range(2):

        def load(index, carry, slot=slot):
            if early:
                pltpu.make_async_copy(
                    mixed.at[index, pl.ds(slot * early, early)], full.at[slot, pl.ds(index * old_rows, early)], sems.at[0, slot]
                ).start()
            pltpu.make_async_copy(
                rest.at[index, pl.ds(slot * late, late)], full.at[slot, pl.ds(index * old_rows + early, late)], sems.at[0, slot]
            ).start()
            return carry

        lax.fori_loop(0, count, load, 0)
    blank[...] = jnp.zeros(blank.shape, BF)
    for slot in range(2):
        whole = full.at[slot, pl.ds(0, cached)]
        pltpu.make_async_copy(whole, whole, sems.at[0, slot]).wait()
        length = prior_len[owners[2 * group + slot]]

        def fill(index, carry, slot=slot, length=length):
            pltpu.make_async_copy(
                blank, full.at[slot, pl.ds(length + fresh + index * BLOCK, BLOCK)], sems.at[1, slot]
            ).start()
            return carry

        lax.fori_loop(0, cached // BLOCK, fill, 0)

        def store(index, carry, slot=slot, length=length):
            pltpu.make_async_copy(
                rest.at[index, pl.ds(2 * late + slot * new_rows, new_rows)],
                full.at[slot, pl.ds(length + index * new_rows, new_rows)],
                sems.at[1, slot],
            ).start()
            return carry

        lax.fori_loop(0, count, store, 0)
    for slot in range(2):
        whole = full.at[slot, pl.ds(0, cached + fresh)]
        pltpu.make_async_copy(whole, whole, sems.at[1, slot]).wait()
        for block in range(blocks):
            pltpu.make_async_copy(
                full.at[slot, pl.ds(block * BLOCK, BLOCK)],
                out.at[0, table[(2 * group + slot) * blocks + block]],
                sems.at[2, 0],
            ).start()
    pltpu.make_async_copy(out, out, sems.at[2, 0]).wait()


def pages(slot_map, prior_len, table, mixed, rest, fresh):
    count, _, _, width = mixed.shape
    cached = count * (mixed.shape[1] + rest.shape[1] - 4 * fresh) // 2
    fresh = count * fresh
    return pl.pallas_call(
        pages_kernel,
        out_shape=jax.ShapeDtypeStruct((1, 2 * (cached + fresh) // BLOCK, BLOCK, 2, width), BF),
        in_specs=specs("s", "s", "s", "a", "a"),
        out_specs=specs("a")[0],
        scratch_shapes=[
            pltpu.SMEM((count,), jnp.int32),
            pltpu.VMEM((2, 2 * cached + fresh, 2, width), BF),
            pltpu.VMEM((BLOCK, 2, width), BF),
            pltpu.SemaphoreType.DMA((3, 2)),
        ],
        compiler_params=PARAMS,
        name="pages",
    )(slot_map, prior_len, table, mixed, rest)


def rotary_tables(prior_count, rows):
    lane = jnp.arange(128, dtype=jnp.int32) % HEAD_DIM
    half_rot = ROTARY // 2
    frequency = ROPE_BASE ** (-2.0 * (lane % half_rot).astype(F32) / ROTARY)
    frequency = jnp.where(lane < ROTARY, frequency, 0.0)
    positions = (prior_count + jnp.arange(rows, dtype=jnp.int32)).astype(F32)
    angles = positions[:, None] * frequency[None, :]
    sine = jnp.sin(angles)
    return (
        jnp.cos(angles),
        jnp.where(lane < half_rot, -sine, 0.0),
        jnp.where((lane >= half_rot) & (lane < ROTARY), sine, 0.0),
    )


def exchange(pieces):
    return lax.all_to_all(pieces, "req", split_axis=0, concat_axis=0, tiled=True)


def layer(
    tokens,
    first_gain,
    first_shift,
    project_weight,
    project_bias,
    output_weight,
    second_gain,
    second_shift,
    expand_weight,
    contract_weight,
    prior_cache,
    prior_len,
    slot_map,
    block_table,
):
    count = slot_map.shape[0]
    rows, width = tokens.shape
    half = rows // 2
    cached = prior_cache.shape[1]
    prior_count = prior_len[lax.axis_index("req")]
    top, bottom = tokens[:half], tokens[half:]
    pieces = ring_gather(top, bottom)
    old = exchange(prior_cache.reshape(count, cached // count, 2, width))
    old_keys, old_values = split(prior_cache[0])
    tables = rotary_tables(prior_count, rows)
    queries, new_keys, new_values = project(
        pieces,
        first_gain.reshape(4, width),
        first_shift.reshape(4, width),
        jnp.transpose(project_weight, (1, 0, 2)),
        project_bias,
        tables,
    )
    parts = attend(prior_len, queries, new_keys, new_values, old_keys, old_values, output_weight)
    mixed = mix(slot_map, old, new_keys, new_values, EARLY)
    mixed = exchange(mixed)
    top_sum, bottom_sum = ring_scatter(parts)
    top = (top.astype(F32) + top_sum).astype(BF)
    bottom = (bottom.astype(F32) + bottom_sum).astype(BF)
    expand = jnp.transpose(expand_weight, (1, 0, 2))
    top, bottom, expand = lax.optimization_barrier((top, bottom, expand))
    pieces = ring_gather(top, bottom)
    parts = feed_forward(pieces, second_gain.reshape(4, width), second_shift.reshape(4, width), expand, contract_weight)
    rest = reorder(slot_map, old, mixed, rows // count)
    rest = exchange(rest)
    top_sum, bottom_sum = ring_scatter(parts)
    result = jnp.concatenate(
        [(top.astype(F32) + top_sum).astype(BF), (bottom.astype(F32) + bottom_sum).astype(BF)], axis=0
    )
    page_pool = pages(slot_map, prior_len, block_table.reshape(-1), mixed, rest, rows // count)
    return (result, page_pool)


def solution(mesh):
    return jax.shard_map(
        layer,
        mesh=mesh,
        in_specs=(
            P("req", "tp"),
            P(),
            P(),
            P(None, None, "tp"),
            P(None, "tp"),
            P("tp", None),
            P(),
            P(),
            P(None, None, "tp"),
            P("tp", None),
            P("req", None, None, "tp"),
            P(),
            P(),
            P(),
        ),
        out_specs=(P("req", "tp"), P("req", None, None, None, "tp")),
        check_vma=False,
    )
```

```python
import functools

import jax
import jax.numpy as jnp
from jax import lax
from jax.experimental import pallas as pl
from jax.experimental.pallas import tpu as pltpu
from jax.sharding import PartitionSpec as P


HEAD_DIM = 64
ROTARY = 16
BLOCK = 256
EPSILON = 1e-05
ROPE_BASE = 10000.0
MASK_FILL = -1e30
BF = jnp.bfloat16
F32 = jnp.float32


OFFSETS = (0, 3, 1, 2)
EARLY = 8


def shift_by(value, step):
    return lax.ppermute(value, "tp", [(i, (i + step) % 4) for i in range(4)])


def ring_gather(top, bottom):
    left_top = shift_by(top, 1)
    right_bottom = shift_by(bottom, -1)
    left_bottom = shift_by(bottom, 1)
    right_top = shift_by(top, -1)
    far_top = shift_by(left_top, 1)
    far_bottom = shift_by(right_bottom, -1)
    return (top, bottom, left_top, left_bottom, right_top, right_bottom, far_top, far_bottom)


def ring_scatter(parts):
    own_top, own_bottom, left_top, left_bottom, right_top, right_bottom, far_top, far_bottom = parts
    add = lambda a, b: (a.astype(F32) + b.astype(F32))
    far_top = shift_by(far_top, 1)
    far_bottom = shift_by(far_bottom, -1)
    from_left_bottom = shift_by(right_bottom, 1)
    from_right_top = shift_by(left_top, -1)
    from_left_top = shift_by(add(right_top, far_top).astype(BF), 1)
    from_right_bottom = shift_by(add(left_bottom, far_bottom).astype(BF), -1)
    top = add(own_top, from_right_top) + from_left_top.astype(F32)
    bottom = add(own_bottom, from_left_bottom) + from_right_bottom.astype(F32)
    return top, bottom


def norm_into(normed, pieces, gain, shift, blocks, half):
    width = pieces[0].shape[1]
    total = 4 * width
    step = 64
    for part in range(2):
        refs = pieces[part::2]

        def body(index, carry, refs=refs, part=part):
            at = pl.multiple_of(index * step, step)
            rows = [ref[pl.ds(at, step), :].astype(F32) for ref in refs]
            mean = sum(jnp.sum(row, axis=1, keepdims=True) for row in rows) / total
            rows = [row - mean for row in rows]
            spread = sum(jnp.sum(row * row, axis=1, keepdims=True) for row in rows) / total
            scale = lax.rsqrt(spread + EPSILON)
            for slot, row in enumerate(rows):
                line = blocks[slot]
                value = row * scale * gain[pl.ds(line, 1), :] + shift[pl.ds(line, 1), :]
                normed[pl.ds(part * half + at, step), slot * width : (slot + 1) * width] = value.astype(BF)
            return carry

        lax.fori_loop(0, half // step, body, 0, unroll=2)


def project_kernel(
    o0, o1, l0, l1, r0, r1, f0, f1, gain, shift, weight, bias, cosine, sine_a, sine_b, queries, keys, values, buffer, normed, sems
):
    device = lax.axis_index("tp")
    width = o0.shape[1]
    half = o0.shape[0]
    blocks = [lax.rem(device + offset, 4) for offset in OFFSETS]
    copies = []
    for slot in range(4):
        copies.append(
            pltpu.make_async_copy(
                weight.at[:, pl.ds(blocks[slot] * width, width), :],
                buffer.at[:, pl.ds(slot * width, width), :],
                sems.at[slot],
            )
        )
        copies[-1].start()
    norm_into(normed, (o0, o1, l0, l1, r0, r1, f0, f1), gain, shift, blocks, half)
    for copy in copies:
        copy.wait()
    outs = (queries, keys, values)
    for part in range(2):
        rows = slice(part * half, (part + 1) * half)
        for which in range(3):
            product = jnp.dot(normed[rows, :], buffer[which], preferred_element_type=F32)
            product = product + bias[which : which + 1, :]
            if which == 2:
                outs[which][rows, :] = product.astype(BF)
                continue
            for tile in range(width // 128):
                lanes = slice(tile * 128, (tile + 1) * 128)
                value = product[:, lanes]
                up = pltpu.roll(value, 128 - ROTARY // 2, 1)
                down = pltpu.roll(value, ROTARY // 2, 1)
                turned = value * cosine[rows, :] + up * sine_a[rows, :] + down * sine_b[rows, :]
                if which == 0:
                    turned = turned * HEAD_DIM ** (-0.5)
                outs[which][rows, lanes] = turned.astype(BF)


VMEM = pltpu.MemorySpace.VMEM
SMEM = pltpu.MemorySpace.SMEM


def specs(*kinds):
    table = {"v": pl.BlockSpec(memory_space=VMEM), "s": pl.BlockSpec(memory_space=SMEM), "a": pl.BlockSpec(memory_space=pl.ANY)}
    return [table[kind] for kind in kinds]


PARAMS = pltpu.CompilerParams(vmem_limit_bytes=56 * 1024 * 1024)


def project(pieces, gain, shift, weight, bias, tables):
    half, width = pieces[0].shape
    out = jax.ShapeDtypeStruct((2 * half, width), BF)
    return pl.pallas_call(
        project_kernel,
        out_shape=(out, out, out),
        in_specs=specs(*"v" * 8, "v", "v", "a", "v", "v", "v", "v"),
        out_specs=tuple(specs("v", "v", "v")),
        scratch_shapes=[
            pltpu.VMEM((3, 4 * width, width), BF),
            pltpu.VMEM((2 * half, 4 * width), BF),
            pltpu.SemaphoreType.DMA((4,)),
        ],
        compiler_params=PARAMS,
        name="project",
    )(*pieces, gain, shift, weight, bias, *tables)


def attend_kernel(lengths, queries, new_keys, new_values, old_keys, old_values, weight, *refs):
    outs, (buffer, mixed, sems) = refs[:8], refs[8:]
    device = lax.axis_index("tp")
    prior = lengths[lax.axis_index("req")]
    rows_all, width = queries.shape
    cached = old_keys.shape[0]
    blocks = [lax.rem(device + offset, 4) for offset in OFFSETS]
    copies = []
    for slot in range(4):
        copies.append(
            pltpu.make_async_copy(
                weight.at[:, pl.ds(blocks[slot] * width, width)], buffer.at[:, slot * width : (slot + 1) * width], sems.at[slot]
            )
        )
        copies[-1].start()
    step = 256
    contract = (((1,), (1,)), ((), ()))
    for part in range(rows_all // step):
        rows = slice(part * step, (part + 1) * step)
        seen = (part + 1) * step

        def body(pair, carry, rows=rows, seen=seen, part=part):
            lanes = pl.ds(pl.multiple_of(pair * 128, 128), 128)
            query = queries[rows, lanes]
            old_key, new_key = old_keys[:, lanes], new_keys[:seen, lanes]
            ones = jnp.ones((cached, 128), BF)
            old_value = jnp.concatenate([old_values[:, lanes], ones], axis=1)
            new_value = jnp.concatenate([new_values[:seen, lanes], ones[:seen]], axis=1)
            lane = lax.broadcasted_iota(jnp.int32, (step, 128), 1)
            old_allowed = lax.broadcasted_iota(jnp.int32, (1, cached), 1) < prior
            allowed = lax.broadcasted_iota(jnp.int32, (step, step), 1) <= lax.broadcasted_iota(jnp.int32, (step, step), 0)
            results = []
            for head in range(2):
                own = (lane < HEAD_DIM) if head == 0 else (lane >= HEAD_DIM)
                masked = jnp.where(own, query, jnp.zeros((), BF))
                old_score = lax.dot_general(masked, old_key, contract, preferred_element_type=F32)
                new_score = lax.dot_general(masked, new_key, contract, preferred_element_type=F32)
                scores = [jnp.where(old_allowed, old_score, MASK_FILL)]
                rows_of = [old_value]
                if part:
                    scores.append(new_score[:, : part * step])
                    rows_of.append(new_value[: part * step])
                scores.append(jnp.where(allowed, new_score[:, part * step :], MASK_FILL))
                rows_of.append(new_value[part * step :])
                highest = functools.reduce(jnp.maximum, [jnp.max(score, axis=1, keepdims=True) for score in scores])
                value = sum(
                    jnp.dot(jnp.exp(score - highest).astype(BF), these, preferred_element_type=F32)
                    for score, these in zip(scores, rows_of)
                )
                results.append(value[:, :128] / value[:, 128:])
            mixed[rows, lanes] = jnp.where(lane < HEAD_DIM, results[0], results[1]).astype(BF)
            return carry

        lax.fori_loop(0, width // 128, body, 0, unroll=4)
    for copy in copies:
        copy.wait()
    for part in range(rows_all // step):
        rows = slice(part * step, (part + 1) * step)
        for slot in range(4):
            product = jnp.dot(mixed[rows, :], buffer[:, slot * width : (slot + 1) * width], preferred_element_type=F32)
            outs[2 * slot + part][...] = product.astype(BF)


def attend(lengths, queries, new_keys, new_values, old_keys, old_values, weight):
    rows, width = queries.shape
    return pl.pallas_call(
        attend_kernel,
        out_shape=(jax.ShapeDtypeStruct((rows // 2, width), BF),) * 8,
        in_specs=specs("s", "v", "v", "v", "v", "v", "a"),
        out_specs=tuple(specs(*"v" * 8)),
        scratch_shapes=[pltpu.VMEM((width, 4 * width), BF), pltpu.VMEM((rows, width), BF), pltpu.SemaphoreType.DMA((4,))],
        compiler_params=PARAMS,
        name="attend",
    )(lengths, queries, new_keys, new_values, old_keys, old_values, weight)


def forward_kernel(o0, o1, l0, l1, r0, r1, f0, f1, gain, shift, expand, contract, *refs):
    outs, (expand_buffer, contract_buffer, normed, sems) = refs[:8], refs[8:]
    device = lax.axis_index("tp")
    half, width = o0.shape
    blocks = [lax.rem(device + offset, 4) for offset in OFFSETS]
    copies = []
    for slot in range(4):
        copies.append(
            pltpu.make_async_copy(
                expand.at[:, pl.ds(blocks[slot] * width, width), :],
                expand_buffer.at[:, slot * width : (slot + 1) * width, :],
                sems.at[0, slot],
            )
        )
    for slot in range(4):
        copies.append(
            pltpu.make_async_copy(
                contract.at[:, pl.ds(blocks[slot] * width, width)],
                contract_buffer.at[:, slot * width : (slot + 1) * width],
                sems.at[1, slot],
            )
        )
    for copy in copies:
        copy.start()
    norm_into(normed, (o0, o1, l0, l1, r0, r1, f0, f1), gain, shift, blocks, half)
    for copy in copies:
        copy.wait()
    for part in range(2):
        rows = slice(part * half, (part + 1) * half)
        gate = jnp.dot(normed[rows, :], expand_buffer[0], preferred_element_type=F32)
        up = jnp.dot(normed[rows, :], expand_buffer[1], preferred_element_type=F32)
        hidden = (gate / (1.0 + jnp.exp(-gate)) * up).astype(BF)
        for slot in range(4):
            product = jnp.dot(hidden, contract_buffer[:, slot * width : (slot + 1) * width], preferred_element_type=F32)
            outs[2 * slot + part][...] = product.astype(BF)


def feed_forward(pieces, gain, shift, expand, contract):
    half, width = pieces[0].shape
    hidden = expand.shape[2]
    return pl.pallas_call(
        forward_kernel,
        out_shape=(jax.ShapeDtypeStruct((half, width), BF),) * 8,
        in_specs=specs(*"v" * 8, "v", "v", "a", "a"),
        out_specs=tuple(specs(*"v" * 8)),
        scratch_shapes=[
            pltpu.VMEM((2, 4 * width, hidden), BF),
            pltpu.VMEM((hidden, 4 * width), BF),
            pltpu.VMEM((2 * half, 4 * width), BF),
            pltpu.SemaphoreType.DMA((2, 4)),
        ],
        compiler_params=PARAMS,
        name="feed_forward",
    )(*pieces, gain, shift, expand, contract)


def split_kernel(cache, keys, values):
    _, _, width = cache.shape
    step = 128
    row = lax.broadcasted_iota(jnp.int32, (2 * step, 2 * step), 0)
    column = lax.broadcasted_iota(jnp.int32, (2 * step, 2 * step), 1)
    source = jnp.where(row < step, 2 * row, 2 * (row - step) + 1)
    chosen = jnp.where(column == source, 1.0, 0.0).astype(BF)

    def body(index, carry):
        at = pl.multiple_of(index * step, step)
        pair = cache[pl.ds(at, step)].reshape(2 * step, width)
        parted = jnp.dot(chosen, pair, preferred_element_type=F32).astype(BF)
        keys[pl.ds(at, step), :] = parted[:step]
        values[pl.ds(at, step), :] = parted[step:]
        return carry

    lax.fori_loop(0, cache.shape[0] // step, body, 0)


def split(cache):
    rows, _, width = cache.shape
    out = jax.ShapeDtypeStruct((rows, width), BF)
    return pl.pallas_call(
        split_kernel,
        out_shape=(out, out),
        in_specs=specs("v"),
        out_specs=tuple(specs("v", "v")),
        compiler_params=PARAMS,
        name="split",
    )(cache)


def find_owners(slot_map, owners):
    def body(index, carry):
        owners[slot_map[index]] = index
        return carry

    lax.fori_loop(0, slot_map.shape[0], body, 0)


def send_old(pieces, owners, out, sem, first, rows):
    half = pieces.shape[3] // 2

    def send(slot, carry):
        group = slot // 2
        for side in range(2):
            pltpu.make_async_copy(
                pieces.at[owners[slot], pl.ds(first, rows), :, side * half : (side + 1) * half],
                out.at[2 * group + side, pl.ds((slot - 2 * group) * rows, rows)],
                sem,
            ).start()
        return carry

    lax.fori_loop(0, pieces.shape[0], send, 0)


def mix_kernel(slot_map, pieces, keys, values, out, owners, stage, sems):
    count = pieces.shape[0]
    half = pieces.shape[3] // 2
    fresh = keys.shape[0] // count
    early = out.shape[1] // 2 - fresh
    find_owners(slot_map, owners)
    send_old(pieces, owners, out, sems.at[0], 0, early)

    def weave(slot, carry):
        at = pl.multiple_of(slot * fresh, fresh)
        for side in range(2):
            lanes = slice(side * half, (side + 1) * half)
            stage[slot, side * fresh : (side + 1) * fresh, 0, :] = keys[pl.ds(at, fresh), lanes]
            stage[slot, side * fresh : (side + 1) * fresh, 1, :] = values[pl.ds(at, fresh), lanes]
        return carry

    lax.fori_loop(0, count, weave, 0)
    last = pltpu.make_async_copy(stage, out.at[:, 2 * early :], sems.at[1])
    last.start()
    first = out.at[:, : 2 * early]
    pltpu.make_async_copy(first, first, sems.at[0]).wait()
    last.wait()


def mix(slot_map, pieces, keys, values, early):
    count, _, _, width = pieces.shape
    fresh = keys.shape[0] // count
    return pl.pallas_call(
        mix_kernel,
        out_shape=jax.ShapeDtypeStruct((count, 2 * early + 2 * fresh, 2, width // 2), BF),
        in_specs=specs("s", "v", "v", "v"),
        out_specs=specs("a")[0],
        scratch_shapes=[
            pltpu.SMEM((count,), jnp.int32),
            pltpu.VMEM((count, 2 * fresh, 2, width // 2), BF),
            pltpu.SemaphoreType.DMA((2,)),
        ],
        compiler_params=PARAMS,
        name="mix",
    )(slot_map, pltpu.with_memory_space_constraint(pieces, VMEM), keys, values)


def reorder_kernel(slot_map, pieces, mixed, out, owners, stage, sems):
    count, rows, _, _ = pieces.shape
    fresh = stage.shape[1] // 2
    late = out.shape[1] // 2 - fresh
    early = rows - late
    find_owners(slot_map, owners)

    def load(slot, carry):
        pltpu.make_async_copy(mixed.at[owners[slot], pl.ds(2 * early, 2 * fresh)], stage.at[slot], sems.at[0]).start()
        return carry

    lax.fori_loop(0, count, load, 0)
    send_old(pieces, owners, out, sems.at[1], early, late)
    pltpu.make_async_copy(stage, stage, sems.at[0]).wait()

    def send(slot, carry):
        group = slot // 2
        for side in range(2):
            pltpu.make_async_copy(
                stage.at[slot, pl.ds(side * fresh, fresh)],
                out.at[2 * group + side, pl.ds(2 * late + (slot - 2 * group) * fresh, fresh)],
                sems.at[2],
            ).start()
        return carry

    lax.fori_loop(0, count, send, 0)
    first, last = out.at[:, : 2 * late], out.at[:, 2 * late :]
    pltpu.make_async_copy(first, first, sems.at[1]).wait()
    pltpu.make_async_copy(last, last, sems.at[2]).wait()


def reorder(slot_map, pieces, mixed, fresh):
    count, rows, _, width = pieces.shape
    late = rows - (mixed.shape[1] // 2 - fresh)
    return pl.pallas_call(
        reorder_kernel,
        out_shape=jax.ShapeDtypeStruct((count, 2 * late + 2 * fresh, 2, width // 2), BF),
        in_specs=specs("s", "v", "v"),
        out_specs=specs("a")[0],
        scratch_shapes=[
            pltpu.SMEM((count,), jnp.int32),
            pltpu.VMEM((count, 2 * fresh, 2, width // 2), BF),
            pltpu.SemaphoreType.DMA((3,)),
        ],
        compiler_params=PARAMS,
        name="reorder",
    )(slot_map, pltpu.with_memory_space_constraint(pieces, VMEM), pltpu.with_memory_space_constraint(mixed, VMEM))


def pages_kernel(slot_map, prior_len, table, mixed, rest, out, owners, full, blank, sems):
    count = mixed.shape[0]
    blocks = out.shape[1] // 2
    new_rows = (mixed.shape[1] + rest.shape[1]) // 2 - blocks * BLOCK // count
    early = mixed.shape[1] // 2 - new_rows
    late = rest.shape[1] // 2 - new_rows
    old_rows = early + late
    cached, fresh = count * old_rows, count * new_rows
    group = lax.axis_index("req") // 2
    find_owners(slot_map, owners)
    for slot in range(2):

        def load(index, carry, slot=slot):
            if early:
                pltpu.make_async_copy(
                    mixed.at[index, pl.ds(slot * early, early)], full.at[slot, pl.ds(index * old_rows, early)], sems.at[0, slot]
                ).start()
            pltpu.make_async_copy(
                rest.at[index, pl.ds(slot * late, late)], full.at[slot, pl.ds(index * old_rows + early, late)], sems.at[0, slot]
            ).start()
            return carry

        lax.fori_loop(0, count, load, 0)
    blank[...] = jnp.zeros(blank.shape, BF)
    for slot in range(2):
        whole = full.at[slot, pl.ds(0, cached)]
        pltpu.make_async_copy(whole, whole, sems.at[0, slot]).wait()
        length = prior_len[owners[2 * group + slot]]

        def fill(index, carry, slot=slot, length=length):
            pltpu.make_async_copy(
                blank, full.at[slot, pl.ds(length + fresh + index * BLOCK, BLOCK)], sems.at[1, slot]
            ).start()
            return carry

        lax.fori_loop(0, cached // BLOCK, fill, 0)

        def store(index, carry, slot=slot, length=length):
            pltpu.make_async_copy(
                rest.at[index, pl.ds(2 * late + slot * new_rows, new_rows)],
                full.at[slot, pl.ds(length + index * new_rows, new_rows)],
                sems.at[1, slot],
            ).start()
            return carry

        lax.fori_loop(0, count, store, 0)
    for slot in range(2):
        whole = full.at[slot, pl.ds(0, cached + fresh)]
        pltpu.make_async_copy(whole, whole, sems.at[1, slot]).wait()
        for block in range(blocks):
            pltpu.make_async_copy(
                full.at[slot, pl.ds(block * BLOCK, BLOCK)],
                out.at[0, table[(2 * group + slot) * blocks + block]],
                sems.at[2, 0],
            ).start()
    pltpu.make_async_copy(out, out, sems.at[2, 0]).wait()


def pages(slot_map, prior_len, table, mixed, rest, fresh):
    count, _, _, width = mixed.shape
    cached = count * (mixed.shape[1] + rest.shape[1] - 4 * fresh) // 2
    fresh = count * fresh
    return pl.pallas_call(
        pages_kernel,
        out_shape=jax.ShapeDtypeStruct((1, 2 * (cached + fresh) // BLOCK, BLOCK, 2, width), BF),
        in_specs=specs("s", "s", "s", "a", "v"),
        out_specs=specs("a")[0],
        scratch_shapes=[
            pltpu.SMEM((count,), jnp.int32),
            pltpu.VMEM((2, 2 * cached + fresh, 2, width), BF),
            pltpu.VMEM((BLOCK, 2, width), BF),
            pltpu.SemaphoreType.DMA((3, 2)),
        ],
        compiler_params=PARAMS,
        name="pages",
    )(slot_map, prior_len, table, mixed, pltpu.with_memory_space_constraint(rest, VMEM))


def rotary_tables(prior_count, rows):
    lane = jnp.arange(128, dtype=jnp.int32) % HEAD_DIM
    half_rot = ROTARY // 2
    frequency = ROPE_BASE ** (-2.0 * (lane % half_rot).astype(F32) / ROTARY)
    frequency = jnp.where(lane < ROTARY, frequency, 0.0)
    positions = (prior_count + jnp.arange(rows, dtype=jnp.int32)).astype(F32)
    angles = positions[:, None] * frequency[None, :]
    sine = jnp.sin(angles)
    return (
        jnp.cos(angles),
        jnp.where(lane < half_rot, -sine, 0.0),
        jnp.where((lane >= half_rot) & (lane < ROTARY), sine, 0.0),
    )


def exchange(pieces):
    return lax.all_to_all(pieces, "req", split_axis=0, concat_axis=0, tiled=True)


def layer(
    tokens,
    first_gain,
    first_shift,
    project_weight,
    project_bias,
    output_weight,
    second_gain,
    second_shift,
    expand_weight,
    contract_weight,
    prior_cache,
    prior_len,
    slot_map,
    block_table,
):
    count = slot_map.shape[0]
    rows, width = tokens.shape
    half = rows // 2
    cached = prior_cache.shape[1]
    prior_count = prior_len[lax.axis_index("req")]
    top, bottom = tokens[:half], tokens[half:]
    pieces = ring_gather(top, bottom)
    old = exchange(prior_cache.reshape(count, cached // count, 2, width))
    old_keys, old_values = split(prior_cache[0])
    tables = rotary_tables(prior_count, rows)
    queries, new_keys, new_values = project(
        pieces,
        first_gain.reshape(4, width),
        first_shift.reshape(4, width),
        jnp.transpose(project_weight, (1, 0, 2)),
        project_bias,
        tables,
    )
    parts = attend(prior_len, queries, new_keys, new_values, old_keys, old_values, output_weight)
    mixed = mix(slot_map, old, new_keys, new_values, EARLY)
    mixed = exchange(mixed)
    top_sum, bottom_sum = ring_scatter(parts)
    top = (top.astype(F32) + top_sum).astype(BF)
    bottom = (bottom.astype(F32) + bottom_sum).astype(BF)
    expand = jnp.transpose(expand_weight, (1, 0, 2))
    top, bottom, expand = lax.optimization_barrier((top, bottom, expand))
    pieces = ring_gather(top, bottom)
    parts = feed_forward(pieces, second_gain.reshape(4, width), second_shift.reshape(4, width), expand, contract_weight)
    rest = reorder(slot_map, old, mixed, rows // count)
    rest = exchange(rest)
    top_sum, bottom_sum = ring_scatter(parts)
    result = jnp.concatenate(
        [(top.astype(F32) + top_sum).astype(BF), (bottom.astype(F32) + bottom_sum).astype(BF)], axis=0
    )
    page_pool = pages(slot_map, prior_len, block_table.reshape(-1), mixed, rest, rows // count)
    return (result, page_pool)


def solution(mesh):
    return jax.shard_map(
        layer,
        mesh=mesh,
        in_specs=(
            P("req", "tp"),
            P(),
            P(),
            P(None, None, "tp"),
            P(None, "tp"),
            P("tp", None),
            P(),
            P(),
            P(None, None, "tp"),
            P("tp", None),
            P("req", None, None, "tp"),
            P(),
            P(),
            P(),
        ),
        out_specs=(P("req", "tp"), P("req", None, None, None, "tp")),
        check_vma=False,
    )
```
